32 devices in a mesh: dp: 8 (over z, y), mp: 4 (over x, core).
Axes of the slice: x: 2, y: 2, z: 4, core: 2. Of those that a mesh axis runs over, the one named last changes fastest.
Arguments:
- patches: bfloat16 [4096, 1152], P(('dp', 'mp')), may hold values from -600 to 600
- norm_gain: float32 [1152], replicated, may hold values from 0.1 to 1.9
- query_key_value: bfloat16 [1152, 3456], P(None, 'mp'), may hold values from -4 to 4
- output_weight: bfloat16 [1152, 1152], P(None, 'mp'), may hold values from -0.1875 to 0.1875
- embed_weight: bfloat16 [1152, 128], replicated, may hold values from -0.1875 to 0.1875
- query_tokens: bfloat16 [32, 32, 128], P('dp'), may hold values from -6 to 6
- patch_counts: int32 [8], replicated, may hold values from 1 to 512, as said below
- positive_page: int32 [32], P('dp'), may hold values from 0 to 7
- hidden_grad: bfloat16 [4096, 1152], P(('dp', 'mp')), may hold values from -6 to 6
Outputs:
- hidden_out: bfloat16 [4096, 1152], P(('dp', 'mp'))
- patches_grad: bfloat16 [4096, 1152], P(('dp', 'mp'))
- output_weight_grad: float32 [1152, 1152], P('dp', 'mp')
- page_scores: float32 [32, 8], P('dp')
- query_loss: float32 [32], P('dp')
The draws below stay inside these ranges and needn't reach their ends.
Inputs may be any that keep to these rules, and one draw needn't show every extreme that they name: `patch_counts`: pages g*1 to g + 1 - 1 belong to group g; in every draw the pages of some group fill all 512 of its rows.
All inputs are finite; a program needn't handle non-finite values.
Results may differ from the reference program's by a relative error of at most 0.0098.
Values may be sent and summed in bfloat16 or wider, within the bound.
No kernel may reach another device: no remote copies, remote signals or barrier semaphores. Data moves between devices by JAX's collectives and lax.ppermute only.
A program may use at most 64 MiB of HBM per device.

```python
from functools import partial
import jax
import jax.numpy as jnp
from jax import lax

D = 1152
HEADS = 16
HEAD_DIM = 72
EMB = 128
ROWS = 512
PPD = 1
QTOK = 32
MAXPATCH = 512
SLOTS = 4096
PAGES = 8
QUERIES = 32
N_DP = 8
N_MP = 4


def draw_patches(key, part):
    first = jax.random.fold_in(key, 0)
    base = jax.random.normal(first, (SLOTS, D), jnp.float32)
    return jnp.clip(base, -600.0, 600.0).astype(jnp.bfloat16)


def draw_query_key_value(key, part):
    base = jax.random.truncated_normal(key, -3.0, 3.0, (D, HEADS, 3, HEAD_DIM), jnp.float32) * D ** (-0.5)
    return jnp.clip(base, -4.0, 4.0).reshape(D, HEADS * 3 * HEAD_DIM).astype(jnp.bfloat16)


def draw_patch_counts(key, part):
    first, second = jax.random.split(key)
    raw = jax.random.randint(first, (PAGES,), 0, MAXPATCH, dtype=jnp.int32)
    sizes = 1 + raw * raw // MAXPATCH
    full = jax.random.randint(second, (), 0, PAGES // PPD, dtype=jnp.int32)
    group = jnp.arange(PAGES, dtype=jnp.int32) // PPD
    return jnp.where(group == full, MAXPATCH, sizes).astype(jnp.int32)


def plant(values, key, least, high):
    shape = values.shape
    place = [jax.random.randint(jax.random.fold_in(key, axis), (), 0, shape[axis]) for axis in range(len(shape))]
    values = values.at[tuple(place)].set(least)
    longest = shape.index(max(shape))
    place[longest] = (place[longest] + 1) % shape[longest]
    return values.at[tuple(place)].set(high)


def spiked(values, key, source, target, blocks, factor):
    def block_of(dim):
        return (jnp.arange(values.shape[dim]) // (values.shape[dim] // blocks)).reshape((-1,) + (1,) * (values.ndim - 1 - dim))

    first = jax.random.permutation(key, blocks)[block_of(target)]
    second = (block_of(target) + blocks // 2) % blocks
    return jnp.where((block_of(source) == first) | (block_of(source) == second), factor * values, values)


def steps_of(stream_key, extent, shards, smallest, high):
    factor_of = 1.0
    for position, shards_of in shards:
        draws = jax.random.uniform(jax.random.fold_in(jax.random.fold_in(stream_key, 6), position), (shards_of,), jnp.float32, smallest / len(shards), high / len(shards))
        factor_of = factor_of * jnp.repeat(jnp.exp(draws), extent[position] // shards_of).reshape((-1,) + (1,) * (len(extent) - 1 - position))
    return factor_of


def noise(key, dims, deviation, bound, pieces=(), held_as=jnp.bfloat16):
    array = jax.random.normal(key, dims, jnp.float32) * deviation
    if len(pieces) > 0:
        array = steps_of(key, dims, pieces, -0.22, 0.18) * array
    return jnp.clip(array, min=-bound, max=bound).astype(held_as)


def heavy_noise(key, extent, scale, most, shards, heavy, kind=jnp.bfloat16):
    values = scale * jax.random.normal(key, extent, jnp.float32)
    if shards:
        values = values * steps_of(key, extent, shards, -0.22, 0.18)
    return jnp.clip(spiked(values, jax.random.fold_in(key, 3), *heavy), -most, most).astype(kind)


def setup_inputs(seed: int = 0) -> dict:
    arg_keys = jax.random.split(jax.random.key(seed), 10)
    patches = draw_patches(jax.random.fold_in(arg_keys[9], 71), 0)
    norm_gain = jnp.clip(1.0 + 0.18 * jax.random.normal(arg_keys[1], (D,), jnp.float32), 0.1, 1.9)
    query_key_value = draw_query_key_value(jax.random.fold_in(arg_keys[9], 71), 0)
    output_weight = noise(arg_keys[3], (D, HEADS * HEAD_DIM), (HEADS * HEAD_DIM) ** -0.5, 0.1875, ((1, 4),))
    embed_weight = noise(arg_keys[4], (D, EMB), D ** -0.5, 0.1875)
    query_tokens = noise(arg_keys[5], (QUERIES, QTOK, EMB), 1.0, 6.0, ((0, 8),))
    patch_counts = draw_patch_counts(jax.random.fold_in(arg_keys[9], 71), 0)
    positive_page = plant(jax.random.randint(arg_keys[7], (QUERIES,), 0, PAGES), jax.random.fold_in(arg_keys[7], 1), 0, PAGES - 1).astype(jnp.int32)
    hidden_grad = heavy_noise(arg_keys[8], (SLOTS, D), 1.0, 6.0, ((0, 32),), (0, 1, 32, 2.75))
    return {"patches": patches, "norm_gain": norm_gain, "query_key_value": query_key_value, "output_weight": output_weight, "embed_weight": embed_weight, "query_tokens": query_tokens, "patch_counts": patch_counts, "positive_page": positive_page, "hidden_grad": hidden_grad}


def layer_norm(values, gain):
    center = values - lax.optimization_barrier(jnp.mean(values, axis=-1, keepdims=True))
    spread = lax.optimization_barrier(jnp.mean(center * center, axis=-1, keepdims=True))
    return center * lax.rsqrt(spread + 1e-06) * gain

def unit_rows(values):
    return values * lax.rsqrt(lax.optimization_barrier(jnp.sum(values * values, axis=-1, keepdims=True)) + 1e-06)

def page_index(counts_group, rows):
    ends = jnp.cumsum(counts_group).astype(jnp.int32)
    places = jnp.arange(rows, dtype=jnp.int32)
    which = lax.optimization_barrier(jnp.sum((places[:, None] >= ends[None, :]).astype(jnp.int32), axis=1)).astype(jnp.int32)
    live = places < ends[-1]
    return (jnp.where(live, which, -1).astype(jnp.int32), live.astype(jnp.float32))

def mix(form, left, right):
    return jnp.einsum(form, left.astype(jnp.float32), right.astype(jnp.float32))

def head_split(projected, heads):
    rows = projected.shape[0]
    parts = jnp.transpose(projected.reshape(rows, heads, 3, HEAD_DIM), (2, 1, 0, 3))
    return (parts[0], parts[1], parts[2])

def softmax_rows(query_rows, key_rows, allowed):
    scores = mix('hqe,hke->hqk', query_rows, key_rows) * HEAD_DIM ** (-0.5)
    scores = jnp.where(allowed[None], scores, -1e+30)
    largest = lax.optimization_barrier(jnp.max(scores, axis=-1, keepdims=True))
    raised = jnp.exp(scores - largest)
    return raised / lax.optimization_barrier(jnp.sum(raised, axis=-1, keepdims=True))

def attend_rows(query_rows, key_rows, value_rows, allowed, live_rows):
    probs = softmax_rows(query_rows, key_rows, allowed)
    weights = probs.astype(jnp.bfloat16)
    result = mix('hqk,hke->hqe', weights, value_rows)
    return (result * live_rows[None, :, None]).astype(jnp.bfloat16)

def attend_back_rows(query_rows, key_rows, value_rows, allowed, live_rows, grad_rows):
    probs = softmax_rows(query_rows, key_rows, allowed)
    weights = probs.astype(jnp.bfloat16)
    grad_live = jnp.where(live_rows[None, :, None] > 0, grad_rows, jnp.zeros_like(grad_rows))
    grad_prob = mix('hqe,hke->hqk', grad_live, value_rows)
    delta = lax.optimization_barrier(jnp.sum(grad_prob * probs, axis=-1, keepdims=True))
    grad_score = (probs * (grad_prob - delta)).astype(jnp.bfloat16)
    grad_query = (mix('hqk,hke->hqe', grad_score, key_rows) * HEAD_DIM ** (-0.5)).astype(jnp.bfloat16)
    grad_key = mix('hqk,hqe->hke', grad_score, query_rows) * HEAD_DIM ** (-0.5)
    grad_value = mix('hqk,hqe->hke', weights, grad_live)
    return (grad_query, grad_key, grad_value)

def reference(patches, norm_gain, query_key_value, output_weight, embed_weight, query_tokens, patch_counts, positive_page, hidden_grad):
    width = HEADS * HEAD_DIM
    share = width // N_MP
    patch_groups = patches.reshape(N_DP, ROWS, D)
    grad_groups = hidden_grad.reshape(N_DP, ROWS, D)
    count_groups = patch_counts.reshape(N_DP, PPD)
    mixing_parts = query_key_value.reshape(D, N_MP, 3 * share)
    output_parts = output_weight.reshape(D, N_MP, share)

    def one_group(total, inputs):
        patch_rows, grad_rows, count_rows = inputs
        page_of, live = page_index(count_rows, ROWS)
        patch_float = patch_rows.astype(jnp.float32)
        normed_float, norm_back = jax.vjp(partial(layer_norm, gain=norm_gain), patch_float)
        normed = normed_float.astype(jnp.bfloat16)
        projected = jnp.dot(normed, query_key_value, preferred_element_type=jnp.float32).astype(jnp.bfloat16)
        query_all, key_all, value_all = head_split(projected, HEADS)
        allowed = page_of[:, None] == page_of[None, :]
        attended_heads = attend_rows(query_all, key_all, value_all, allowed, live)
        attended = jnp.transpose(attended_heads, (1, 0, 2)).reshape(ROWS, width)
        branches = mix('rmc,dmc->mrd', attended.reshape(ROWS, N_MP, share), output_parts).astype(jnp.bfloat16)
        hidden = (patch_float + lax.optimization_barrier(jnp.sum(branches.astype(jnp.float32), axis=0))).astype(jnp.bfloat16)
        embedded = jnp.dot(hidden, embed_weight, preferred_element_type=jnp.float32)
        page_emb = unit_rows(embedded).astype(jnp.bfloat16)
        grad_attended = jnp.dot(grad_rows, output_weight, preferred_element_type=jnp.float32).astype(jnp.bfloat16)
        grad_heads = jnp.transpose(grad_attended.reshape(ROWS, HEADS, HEAD_DIM), (1, 0, 2))
        grad_query, grad_key, grad_value = attend_back_rows(query_all, key_all, value_all, allowed, live, grad_heads)
        stacked = jnp.stack([grad_query, grad_key.astype(jnp.bfloat16), grad_value.astype(jnp.bfloat16)], axis=0)
        grad_projected = jnp.transpose(stacked, (2, 1, 0, 3)).reshape(ROWS, 3 * width)
        grad_parts = mix('rmc,dmc->mrd', grad_projected.reshape(ROWS, N_MP, 3 * share), mixing_parts).astype(jnp.bfloat16)
        normed_grad = lax.optimization_barrier(jnp.sum(grad_parts.astype(jnp.float32), axis=0))
        patch_grad = (grad_rows.astype(jnp.float32) + norm_back(normed_grad)[0]).astype(jnp.bfloat16)
        term = jnp.dot(grad_rows.T, attended, preferred_element_type=jnp.float32)
        return (total + term, (hidden, patch_grad, page_emb, page_of))
    weight_grad, (hidden, patch_grad, page_emb, page_of) = lax.scan(one_group, jnp.zeros((D, width), jnp.float32), (patch_groups, grad_groups, count_groups))
    query_emb = unit_rows(query_tokens.astype(jnp.float32)).astype(jnp.bfloat16)
    flat = query_emb.reshape(QUERIES * QTOK, EMB)

    def best_group(inputs):
        emb_rows, row_pages = inputs
        similar = jnp.dot(flat, emb_rows.T, preferred_element_type=jnp.float32)
        return jnp.stack([lax.optimization_barrier(jnp.max(jnp.where(row_pages[None, :] == which, similar, -2.0), axis=1)) for which in range(PPD)], axis=1)
    best = lax.map(best_group, (page_emb, page_of))
    scores = lax.optimization_barrier(jnp.sum(best.reshape(N_DP, QUERIES, QTOK, PPD), axis=2))
    scores = jnp.transpose(scores, (1, 0, 2)).reshape(QUERIES, PAGES)
    columns = jnp.arange(PAGES, dtype=jnp.int32)
    chosen = columns[None, :] == positive_page[:, None]
    positive_score = lax.optimization_barrier(jnp.sum(jnp.where(chosen, scores, 0.0), axis=1))
    negative_score = lax.optimization_barrier(jnp.max(jnp.where(chosen, -1e+30, scores), axis=1))
    loss = jax.nn.softplus(negative_score - positive_score)
    return (hidden.reshape(SLOTS, D), patch_grad.reshape(SLOTS, D), weight_grad, scores, loss)
```

```python
from functools import partial
import math

import jax
import jax.numpy as jnp
from jax import lax
from jax.experimental import pallas as pl
from jax.experimental.pallas import tpu as pltpu
from jax.sharding import PartitionSpec as P

HEAD_DIM = 72
LANES = 128
EMB = 128
QTOK = 32
MP = 4
SCALE = HEAD_DIM ** (-0.5)
LOG2E = math.log2(math.e)
F32 = jnp.float32
BF16 = jnp.bfloat16

VMEM = pl.BlockSpec(memory_space=pltpu.VMEM)
SMEM = pl.BlockSpec(memory_space=pltpu.SMEM)
HBM = pl.BlockSpec(memory_space=pl.ANY)


def dot(left, right, left_dim, right_dim):
    return lax.dot_general(
        left, right, (((left_dim,), (right_dim,)), ((), ())), preferred_element_type=F32
    )


def shape(dims, kind):
    return jax.ShapeDtypeStruct(dims, kind)


def cost(flops, size, exps=0):
    return pl.CostEstimate(flops=int(flops), bytes_accessed=int(size), transcendentals=int(exps))


def full(*dims):
    return pl.BlockSpec(dims, lambda *_: (0,) * len(dims))


def place_of(index, model_index, rows_dev):
    return (model_index ^ (index // rows_dev)) * rows_dev + index % rows_dev


def pad_kernel(heads, mixing_ref, output_ref, mixing_pad, output_pad):
    mixing_pad[...] = jnp.zeros_like(mixing_pad)
    output_pad[...] = jnp.zeros_like(output_pad)
    for index in range(3 * heads):
        mixing_pad[:, index * LANES : index * LANES + HEAD_DIM] = mixing_ref[
            :, index * HEAD_DIM : (index + 1) * HEAD_DIM
        ]
    for index in range(heads):
        output_pad[:, index * LANES : index * LANES + HEAD_DIM] = output_ref[
            :, index * HEAD_DIM : (index + 1) * HEAD_DIM
        ]


def pad_weights(mixing, output, heads):
    width = mixing.shape[0]
    return pl.pallas_call(
        partial(pad_kernel, heads),
        out_shape=(
            shape((width, 3 * heads * LANES), BF16),
            shape((output.shape[0], heads * LANES), BF16),
        ),
        in_specs=[VMEM, VMEM],
        out_specs=(VMEM, VMEM),
        cost_estimate=cost(0, 8e6),
        name="pad_weights",
    )(mixing, output)


def forward_kernel(
    heads,
    rows_dev,
    where_ref,
    rows0,
    rows1,
    rows2,
    rows3,
    gain_ref,
    mixing_ref,
    output_ref,
    packed_ref,
    prob_ref,
    attended_ref,
    part0,
    part1,
    part2,
    part3,
    normed,
):
    head = pl.program_id(0)
    rows = rows_dev * MP

    @pl.when(head == 0)
    def _():
        for index, block in enumerate((rows0, rows1, rows2, rows3)):
            values = block[...].astype(F32)
            center = values - jnp.mean(values, axis=-1, keepdims=True)
            spread = jnp.mean(center * center, axis=-1, keepdims=True)
            normed[index * rows_dev : (index + 1) * rows_dev, :] = (
                center * lax.rsqrt(spread + 1e-06) * gain_ref[...]
            ).astype(BF16)

    packed = dot(normed[...], mixing_ref[...], 1, 0).astype(BF16)
    packed_ref[...] = packed
    query = packed[:, :LANES]
    key = packed[:, LANES : 2 * LANES]
    value = packed[:, 2 * LANES :]
    count = where_ref[0]
    model_index = where_ref[1]
    columns = lax.broadcasted_iota(jnp.int32, (1, rows), 1)
    seen = place_of(columns, model_index, rows_dev) < count
    step = rows_dev
    for chunk in range(rows // step):
        low = chunk * step
        score = dot(query[low : low + step], key, 1, 1)
        score = jnp.where(seen, score, -1e30)
        largest = jnp.max(score, axis=-1, keepdims=True)
        raised = jnp.exp2((score - largest) * (SCALE * LOG2E))
        total = jnp.sum(raised, axis=-1, keepdims=True)
        prob = (raised * (1.0 / total)).astype(BF16)
        prob_ref[0, low : low + step, :] = prob
        found = dot(prob, value, 1, 0)
        lines = lax.broadcasted_iota(jnp.int32, (step, 1), 0) + low
        live = place_of(lines, model_index, rows_dev) < count
        found = jnp.where(live, found, 0.0).astype(BF16)
        attended_ref[head, low : low + step, :] = found

    @pl.when(head == heads - 1)
    def _():
        joined = jnp.concatenate([attended_ref[index] for index in range(heads)], axis=1)
        for index, part in enumerate((part0, part1, part2, part3)):
            block = joined[index * rows_dev : (index + 1) * rows_dev]
            part[...] = dot(block, output_ref[...], 1, 1).astype(BF16)


def forward(where, blocks, gain, mixing_pad, output_pad, heads):
    rows_dev, width = blocks[0].shape
    rows = rows_dev * MP
    wide = 3 * LANES
    block = full(rows_dev, width)
    return pl.pallas_call(
        partial(forward_kernel, heads, rows_dev),
        grid=(heads,),
        out_shape=(
            shape((rows, heads * wide), BF16),
            shape((heads, rows, rows), BF16),
            shape((heads, rows, LANES), BF16),
        )
        + (shape((rows_dev, width), BF16),) * MP,
        in_specs=[SMEM]
        + [block] * MP
        + [
            full(1, width),
            pl.BlockSpec((width, wide), lambda head: (0, head)),
            full(width, heads * LANES),
        ],
        out_specs=(
            pl.BlockSpec((rows, wide), lambda head: (0, head)),
            pl.BlockSpec((1, rows, rows), lambda head: (head, 0, 0)),
            full(heads, rows, LANES),
        )
        + (block,) * MP,
        scratch_shapes=[pltpu.VMEM((rows, width), BF16)],
        cost_estimate=cost(3e9, 12e6, heads * rows * rows),
        name="forward_attention",
    )(where, *blocks, gain, mixing_pad, output_pad)


def weight_kernel(
    heads, rows_dev, pieces, where_ref, grad0, grad1, grad2, grad3, attended_ref, *refs
):
    outs, (stacked, result) = refs[: len(refs) - 2], refs[len(refs) - 2 :]
    for index, block in enumerate((grad0, grad1, grad2, grad3)):
        stacked[index * rows_dev : (index + 1) * rows_dev, :] = block[...]
    joined = jnp.concatenate([attended_ref[index] for index in range(heads)], axis=1)
    product = dot(stacked[...], joined, 0, 0)
    for index in range(heads):
        result[:, index * HEAD_DIM : (index + 1) * HEAD_DIM] = product[
            :, index * LANES : index * LANES + HEAD_DIM
        ]
    if pieces == 1:
        outs[0][...] = result[...]
    else:
        share = result.shape[0] // pieces
        mine = where_ref[2]
        for piece, out in enumerate(outs):
            start = pl.multiple_of((mine ^ piece) * share, 16)
            out[...] = result[pl.ds(start, share), :].astype(out.dtype)


def weight_parts(where, grads, attended, pieces):
    rows_dev, width = grads[0].shape
    heads = attended.shape[0]
    share = width // pieces
    narrow = heads * HEAD_DIM
    kinds = [F32] + [BF16] * (pieces - 1)
    return pl.pallas_call(
        partial(weight_kernel, heads, rows_dev, pieces),
        out_shape=tuple(shape((share, narrow), kind) for kind in kinds),
        in_specs=[SMEM] + [VMEM] * (MP + 1),
        out_specs=(VMEM,) * pieces,
        scratch_shapes=[
            pltpu.VMEM((rows_dev * MP, width), BF16),
            pltpu.VMEM((width, narrow), F32),
        ],
        cost_estimate=cost(7e8, 4e6),
        name="weight_parts",
    )(where, *grads, attended)


def backward_kernel(
    heads,
    rows_dev,
    where_ref,
    grad0,
    grad1,
    grad2,
    grad3,
    output_ref,
    packed_ref,
    prob_ref,
    mixing_hbm,
    part0,
    part1,
    part2,
    part3,
    stacked,
    joined,
    mixing,
    sem,
):
    head = pl.program_id(0)
    rows = rows_dev * MP
    fetch = pltpu.make_async_copy(mixing_hbm, mixing, sem)

    @pl.when(head == 0)
    def _():
        fetch.start()
        for index, block in enumerate((grad0, grad1, grad2, grad3)):
            stacked[index * rows_dev : (index + 1) * rows_dev, :] = block[...]

    count = where_ref[0]
    model_index = where_ref[1]
    lines = lax.broadcasted_iota(jnp.int32, (rows, 1), 0)
    live = place_of(lines, model_index, rows_dev) < count
    flow = dot(stacked[...], output_ref[...], 1, 0)
    flow = jnp.where(live, flow, 0.0).astype(BF16)
    query = packed_ref[:, :LANES]
    key = packed_ref[:, LANES : 2 * LANES]
    value = packed_ref[:, 2 * LANES :]
    step = rows // 2
    grad_key = jnp.zeros((rows, LANES), F32)
    grad_value = jnp.zeros((rows, LANES), F32)
    grad_query = []
    for low in range(0, rows, step):
        part = flow[low : low + step]
        weights = prob_ref[0, low : low + step, :]
        prob = weights.astype(F32)
        grad_prob = dot(part, value, 1, 1)
        delta = jnp.sum(grad_prob * prob, axis=-1, keepdims=True)
        grad_score = (prob * (grad_prob - delta)).astype(BF16)
        grad_query.append((dot(grad_score, key, 1, 0) * SCALE).astype(BF16))
        grad_key += dot(grad_score, query[low : low + step], 0, 0)
        grad_value += dot(weights, part, 0, 0)
    joined[head, :, :LANES] = jnp.concatenate(grad_query, axis=0)
    joined[head, :, LANES : 2 * LANES] = (grad_key * SCALE).astype(BF16)
    joined[head, :, 2 * LANES :] = grad_value.astype(BF16)

    @pl.when(head == heads - 1)
    def _():
        fetch.wait()
        everything = jnp.concatenate([joined[index] for index in range(heads)], axis=1)
        for index, part in enumerate((part0, part1, part2, part3)):
            block = everything[index * rows_dev : (index + 1) * rows_dev]
            part[...] = dot(block, mixing[...], 1, 1).astype(BF16)


def backward(where, grads, output_pad, packed, probs, mixing_pad, heads):
    rows_dev, width = grads[0].shape
    rows = rows_dev * MP
    wide = 3 * LANES
    block = full(rows_dev, width)
    return pl.pallas_call(
        partial(backward_kernel, heads, rows_dev),
        grid=(heads,),
        out_shape=(shape((rows_dev, width), BF16),) * MP,
        in_specs=[SMEM]
        + [block] * MP
        + [
            pl.BlockSpec((width, LANES), lambda head: (0, head)),
            pl.BlockSpec((rows, wide), lambda head: (0, head)),
            pl.BlockSpec((1, rows, rows), lambda head: (head, 0, 0)),
            HBM,
        ],
        out_specs=(block,) * MP,
        scratch_shapes=[
            pltpu.VMEM((rows, width), BF16),
            pltpu.VMEM((heads, rows, wide), BF16),
            pltpu.VMEM((width, heads * wide), BF16),
            pltpu.SemaphoreType.DMA,
        ],
        cost_estimate=cost(6e9, 12e6),
        name="backward_attention",
    )(where, *grads, output_pad, packed, probs, mixing_pad)


def score_kernel(
    rows_dev, where_ref, patch_ref, part_ref, near_ref, far_ref, embed_ref, tokens_ref,
    hidden_ref, best_ref, page_emb
):
    @pl.when(pl.program_id(0) == 0)
    def _():
        mixed = part_ref[...].astype(F32) + near_ref[...].astype(F32) + far_ref[...].astype(F32)
        hidden = (patch_ref[...].astype(F32) + mixed).astype(BF16)
        hidden_ref[...] = hidden
        embedded = dot(hidden, embed_ref[...], 1, 0)
        page_emb[...] = (
            embedded
            * lax.rsqrt(jnp.sum(embedded * embedded, axis=-1, keepdims=True) + 1e-06)
        ).astype(BF16)

    similar = dot(page_emb[...], tokens_ref[...], 1, 1)
    lines = lax.broadcasted_iota(jnp.int32, (rows_dev, 1), 0) + where_ref[1] * rows_dev
    similar = jnp.where(lines < where_ref[0], similar, -2.0)
    best_ref[...] = jnp.max(similar, axis=0, keepdims=True)


def hidden_and_best(where, patches, part, near, far, embed_weight, tokens):
    rows_dev, width = patches.shape
    size = tokens.shape[0]
    chunk = math.gcd(size, 1024)
    block = full(rows_dev, width)
    return pl.pallas_call(
        partial(score_kernel, rows_dev),
        grid=(size // chunk,),
        out_shape=(shape((rows_dev, width), BF16), shape((1, size), F32)),
        in_specs=[SMEM]
        + [block] * 4
        + [full(width, EMB), pl.BlockSpec((chunk, EMB), lambda index: (index, 0))],
        out_specs=(block, pl.BlockSpec((1, chunk), lambda index: (0, index))),
        scratch_shapes=[pltpu.VMEM((rows_dev, EMB), BF16)],
        cost_estimate=cost(1e8, 2e6),
        name="hidden_and_best",
    )(where, patches, part, near, far, embed_weight, tokens)


def norm_back_kernel(patch_ref, gain_ref, grad_ref, part_ref, near_ref, far_ref, out_ref):
    values = patch_ref[...].astype(F32)
    center = values - jnp.mean(values, axis=-1, keepdims=True)
    spread = jnp.mean(center * center, axis=-1, keepdims=True)
    inverse = lax.rsqrt(spread + 1e-06)
    flow = part_ref[...].astype(F32) + near_ref[...].astype(F32) + far_ref[...].astype(F32)
    flow = flow * gain_ref[...]
    along = jnp.mean(flow * center, axis=-1, keepdims=True)
    level = jnp.mean(flow, axis=-1, keepdims=True)
    result = inverse * (flow - level - center * (inverse * inverse * along))
    out_ref[...] = (grad_ref[...].astype(F32) + result).astype(BF16)


def norm_back(patches, gain, grads, part, near, far):
    return pl.pallas_call(
        norm_back_kernel,
        out_shape=shape(patches.shape, BF16),
        in_specs=[VMEM] * 6,
        out_specs=VMEM,
        cost_estimate=cost(3e6, 2e6),
        name="norm_back",
    )(patches, gain, grads, part, near, far)


def unit_rows(values):
    return values * lax.rsqrt(jnp.sum(values * values, axis=-1, keepdims=True) + 1e-06)


def swap(values, axis, distance):
    size = lax.axis_size(axis)
    return lax.ppermute(values, axis, [(index, index ^ distance) for index in range(size)])


def scatter_sum(parts):
    part0, part1, part2, part3 = parts
    relayed = swap(part3, "mp", 1)
    near = swap(part1, "mp", 1)
    far = swap((part2.astype(F32) + relayed.astype(F32)).astype(BF16), "mp", 2)
    return part0, near, far


def body(
    patches,
    norm_gain,
    query_key_value,
    output_weight,
    embed_weight,
    query_tokens,
    patch_counts,
    positive_page,
    hidden_grad,
):
    model_index = lax.axis_index("mp")
    data_index = lax.axis_index("dp")
    data_size = lax.axis_size("dp")
    few = data_size == 8
    heads = output_weight.shape[1] // HEAD_DIM
    gain = norm_gain.reshape(1, -1)
    count = lax.dynamic_index_in_dim(patch_counts, data_index, 0, keepdims=False)
    where = jnp.stack([count, model_index, data_index]).astype(jnp.int32)

    rows1 = swap(patches, "mp", 1)
    rows2 = swap(patches, "mp", 2)
    rows3 = swap(rows2, "mp", 1)
    grads1 = swap(hidden_grad, "mp", 1)
    late_grad, _ = lax.optimization_barrier((hidden_grad, rows2))
    grads2 = swap(late_grad, "mp", 2)
    grads3 = swap(grads2, "mp", 1)
    grads = (hidden_grad, grads1, grads2, grads3)

    local = query_tokens.shape[0]
    query_emb = unit_rows(query_tokens.astype(F32)).astype(BF16).reshape(local * QTOK, EMB)
    if few:
        pieces = [query_emb] + [swap(query_emb, "dp", index) for index in range(1, data_size)]
        tokens = jnp.concatenate(pieces, axis=0)
    else:
        tokens = lax.all_gather(query_emb, "dp", axis=0, tiled=True)

    mixing_pad, output_pad = pad_weights(query_key_value, output_weight, heads)
    packed, probs, attended, *parts = forward(
        where, (patches, rows1, rows2, rows3), gain, mixing_pad, output_pad, heads
    )
    hidden, best = hidden_and_best(where, patches, *scatter_sum(parts), embed_weight, tokens)

    if few:
        mine, *others = weight_parts(where, grads, attended, data_size)
        weight_grad = mine
        for index, other in enumerate(others):
            weight_grad = weight_grad + swap(other, "dp", index + 1).astype(F32)
    else:
        (whole,) = weight_parts(where, grads, attended, 1)
        weight_grad = lax.psum_scatter(whole, "dp", scatter_dimension=0, tiled=True)

    grad_parts = backward(where, grads, output_pad, packed, probs, mixing_pad, heads)
    patch_grad = norm_back(patches, gain, hidden_grad, *scatter_sum(grad_parts))

    best = jnp.maximum(best, swap(best, "mp", 1))
    best = jnp.maximum(best, swap(best, "mp", 2))
    part_scores = jnp.sum(best.reshape(-1, QTOK), axis=1)
    if few:
        pieces = part_scores.reshape(data_size, local)
        found = [pieces[0]]
        for index in range(1, data_size):
            found.append(swap(pieces[index], "dp", index))
        found = jnp.stack(found, axis=1)
        order = jnp.arange(data_size, dtype=jnp.int32)
        chosen = (order[:, None] ^ data_index) == order[None, :]
        my_scores = jnp.sum(jnp.where(chosen[None], found[:, :, None], 0.0), axis=1)
    else:
        every = lax.all_gather(part_scores.reshape(-1, 1), "dp", axis=1, tiled=True)
        my_scores = lax.dynamic_slice_in_dim(every, data_index * local, local, 0)
    columns = jnp.arange(my_scores.shape[1], dtype=jnp.int32)
    chosen = columns[None, :] == positive_page[:, None]
    positive_score = jnp.sum(jnp.where(chosen, my_scores, 0.0), axis=1)
    negative_score = jnp.max(jnp.where(chosen, -1e30, my_scores), axis=1)
    loss = jax.nn.softplus(negative_score - positive_score)
    return (hidden, patch_grad, weight_grad, my_scores, loss)


def solution(mesh):
    return jax.shard_map(
        body,
        mesh=mesh,
        in_specs=(
            P(("dp", "mp"), None),
            P(),
            P(None, "mp"),
            P(None, "mp"),
            P(),
            P("dp", None, None),
            P(),
            P("dp"),
            P(("dp", "mp"), None),
        ),
        out_specs=(
            P(("dp", "mp"), None),
            P(("dp", "mp"), None),
            P("dp", "mp"),
            P("dp", None),
            P("dp"),
        ),
        check_vma=False,
    )
```

```python
from functools import partial
import math

import jax
import jax.numpy as jnp
from jax import lax
from jax.experimental import pallas as pl
from jax.experimental.pallas import tpu as pltpu
from jax.sharding import PartitionSpec as P

HEAD_DIM = 72
LANES = 128
EMB = 128
QTOK = 32
MP = 4
SCALE = HEAD_DIM ** (-0.5)
LOG2E = math.log2(math.e)
F32 = jnp.float32
BF16 = jnp.bfloat16

VMEM = pl.BlockSpec(memory_space=pltpu.VMEM)
SMEM = pl.BlockSpec(memory_space=pltpu.SMEM)
HBM = pl.BlockSpec(memory_space=pl.ANY)


def dot(left, right, left_dim, right_dim):
    return lax.dot_general(
        left, right, (((left_dim,), (right_dim,)), ((), ())), preferred_element_type=F32
    )


def shape(dims, kind):
    return jax.ShapeDtypeStruct(dims, kind)


def cost(flops, size, exps=0):
    return pl.CostEstimate(flops=int(flops), bytes_accessed=int(size), transcendentals=int(exps))


def grant(mebibytes):
    return pltpu.CompilerParams(vmem_limit_bytes=mebibytes * 1024 * 1024)


def full(*dims):
    return pl.BlockSpec(dims, lambda *_: (0,) * len(dims))


def unit_rows(values):
    return values * lax.rsqrt(jnp.sum(values * values, axis=-1, keepdims=True) + 1e-06)


def place_of(index, model_index, rows_dev):
    return (model_index ^ (index // rows_dev)) * rows_dev + index % rows_dev


def prepare_kernel(heads, mixing_ref, output_ref, tokens_ref, mixing_pad, output_pad, unit_ref):
    def spread(source, target, index):
        target[index * LANES : index * LANES + HEAD_DIM, :] = source[
            index * HEAD_DIM : (index + 1) * HEAD_DIM, :
        ]
        target[index * LANES + HEAD_DIM : (index + 1) * LANES, :] = jnp.zeros(
            (LANES - HEAD_DIM, target.shape[1]), BF16
        )

    values = tokens_ref[...].astype(F32)
    unit_ref[...] = unit_rows(values).astype(BF16)
    for index in range(3 * heads):
        spread(mixing_ref, mixing_pad, index)
    for index in range(heads):
        spread(output_ref, output_pad, index)


def prepare(mixing, output, tokens, heads):
    width = mixing.shape[1]
    return pl.pallas_call(
        partial(prepare_kernel, heads),
        out_shape=(
            shape((3 * heads * LANES, width), BF16),
            shape((heads * LANES, width), BF16),
            shape(tokens.shape, BF16),
        ),
        in_specs=[VMEM] * 3,
        out_specs=(VMEM,) * 3,
        cost_estimate=cost(0, 8e6),
        name="prepare",
        compiler_params=grant(24),
    )(mixing, output, tokens)


def hand_out(product, keep0, keep2, send):
    size = keep0.shape[0]
    keep0[...] = product[:size].astype(BF16)
    send[:size, :] = product[size : 2 * size].astype(BF16)
    keep2[...] = product[2 * size : 3 * size].astype(BF16)
    send[size:, :] = product[3 * size :].astype(BF16)


def forward_kernel(
    heads,
    rows_dev,
    counts_ref,
    rows0,
    rows1,
    rows2,
    rows3,
    gain_ref,
    mixing_ref,
    output_ref,
    packed_ref,
    prob_ref,
    attended_ref,
    keep0,
    keep2,
    send,
    normed,
):
    head = pl.program_id(0)
    rows = rows_dev * MP

    @pl.when(head == 0)
    def _():
        for index, block in enumerate((rows0, rows1, rows2, rows3)):
            values = block[...].astype(F32)
            center = values - jnp.mean(values, axis=-1, keepdims=True)
            spread = jnp.mean(center * center, axis=-1, keepdims=True)
            normed[index * rows_dev : (index + 1) * rows_dev, :] = (
                center * lax.rsqrt(spread + 1e-06) * gain_ref[...]
            ).astype(BF16)

    packed = dot(normed[...], mixing_ref[...], 1, 1).astype(BF16)
    packed_ref[...] = packed
    query = packed[:, :LANES]
    key = packed[:, LANES : 2 * LANES]
    value = packed[:, 2 * LANES :]
    count = counts_ref[lax.axis_index("dp")]
    model_index = lax.axis_index("mp")
    columns = lax.broadcasted_iota(jnp.int32, (1, rows), 1)
    seen = place_of(columns, model_index, rows_dev) < count
    step = rows_dev
    for chunk in range(rows // step):
        low = chunk * step
        score = dot(query[low : low + step], key, 1, 1)
        score = jnp.where(seen, score, -1e30)
        largest = jnp.max(score, axis=-1, keepdims=True)
        raised = jnp.exp2((score - largest) * (SCALE * LOG2E))
        total = jnp.sum(raised, axis=-1, keepdims=True)
        prob = (raised * (1.0 / total)).astype(BF16)
        prob_ref[0, low : low + step, :] = prob
        found = dot(prob, value, 1, 0)
        lines = lax.broadcasted_iota(jnp.int32, (step, 1), 0) + low
        live = place_of(lines, model_index, rows_dev) < count
        found = jnp.where(live, found, 0.0).astype(BF16)
        attended_ref[head, low : low + step, :] = found

    @pl.when(head == heads - 1)
    def _():
        joined = jnp.concatenate([attended_ref[index] for index in range(heads)], axis=1)
        hand_out(dot(joined, output_ref[...], 1, 0), keep0, keep2, send)


def handed_shapes(rows_dev, width):
    kept = shape((rows_dev, width), BF16)
    return (kept, kept, shape((2 * rows_dev, width), BF16))


def forward(counts, blocks, gain, mixing_pad, output_pad, heads):
    rows_dev, width = blocks[0].shape
    rows = rows_dev * MP
    wide = 3 * LANES
    block = full(rows_dev, width)
    return pl.pallas_call(
        partial(forward_kernel, heads, rows_dev),
        grid=(heads,),
        out_shape=(
            shape((rows, heads * wide), BF16),
            shape((heads, rows, rows), BF16),
            shape((heads, rows, LANES), BF16),
        )
        + handed_shapes(rows_dev, width),
        in_specs=[SMEM]
        + [block] * MP
        + [
            full(1, width),
            pl.BlockSpec((wide, width), lambda head: (head, 0)),
            full(heads * LANES, width),
        ],
        out_specs=(
            pl.BlockSpec((rows, wide), lambda head: (0, head)),
            pl.BlockSpec((1, rows, rows), lambda head: (head, 0, 0)),
            full(heads, rows, LANES),
        )
        + (block, block, full(2 * rows_dev, width)),
        scratch_shapes=[pltpu.VMEM((rows, width), BF16)],
        cost_estimate=cost(3e9, 12e6, heads * rows * rows),
        name="forward_attention",
        compiler_params=grant(24),
    )(counts, *blocks, gain, mixing_pad, output_pad)


def weight_kernel(heads, rows_dev, order, grad0, grad1, grad2, grad3, attended_ref, *refs):
    outs, (stacked, result) = refs[: len(refs) - 2], refs[len(refs) - 2 :]
    for index, block in enumerate((grad0, grad1, grad2, grad3)):
        stacked[index * rows_dev : (index + 1) * rows_dev, :] = block[...]
    joined = jnp.concatenate([attended_ref[index] for index in range(heads)], axis=1)
    product = dot(stacked[...], joined, 0, 0)
    for index in range(heads):
        result[:, index * HEAD_DIM : (index + 1) * HEAD_DIM] = product[
            :, index * LANES : index * LANES + HEAD_DIM
        ]
    if order is None:
        outs[0][...] = result[...]
    else:
        mine = lax.axis_index("dp")
        share = result.shape[0] // sum(len(group) for group in order)
        for group, out in zip(order, outs):
            for spot, piece in enumerate(group):
                start = pl.multiple_of((mine ^ piece) * share, 16)
                out[spot * share : (spot + 1) * share, :] = result[
                    pl.ds(start, share), :
                ].astype(out.dtype)


def weight_parts(grads, attended, order):
    rows_dev, width = grads[0].shape
    heads = attended.shape[0]
    narrow = heads * HEAD_DIM
    if order is None:
        outs = (shape((width, narrow), F32),)
    else:
        share = width // sum(len(group) for group in order)
        outs = tuple(
            shape((len(group) * share, narrow), F32 if index == 0 else BF16)
            for index, group in enumerate(order)
        )
    return pl.pallas_call(
        partial(weight_kernel, heads, rows_dev, order),
        out_shape=outs,
        in_specs=[VMEM] * (MP + 1),
        out_specs=(VMEM,) * len(outs),
        scratch_shapes=[
            pltpu.VMEM((rows_dev * MP, width), BF16),
            pltpu.VMEM((width, narrow), F32),
        ],
        cost_estimate=cost(7e8, 4e6),
        name="weight_parts",
        compiler_params=grant(20),
    )(*grads, attended)


def backward_kernel(
    heads,
    last,
    rows_dev,
    counts_ref,
    grad0,
    grad1,
    grad2,
    grad3,
    output_ref,
    packed_ref,
    prob_ref,
    *refs,
):
    head = pl.program_id(0)
    rows = rows_dev * MP
    if last:
        earlier, mixing_hbm, keep0, keep2, send, stacked, joined, mixing, sem = refs
        fetch = pltpu.make_async_copy(mixing_hbm, mixing, sem)
    else:
        joined, stacked = refs

    @pl.when(head == 0)
    def _():
        if last:
            fetch.start()
        for index, block in enumerate((grad0, grad1, grad2, grad3)):
            stacked[index * rows_dev : (index + 1) * rows_dev, :] = block[...]

    count = counts_ref[lax.axis_index("dp")]
    model_index = lax.axis_index("mp")
    lines = lax.broadcasted_iota(jnp.int32, (rows, 1), 0)
    live = place_of(lines, model_index, rows_dev) < count
    flow = dot(stacked[...], output_ref[...], 1, 1)
    flow = jnp.where(live, flow, 0.0).astype(BF16)
    query = packed_ref[:, :LANES]
    key = packed_ref[:, LANES : 2 * LANES]
    value = packed_ref[:, 2 * LANES :]
    step = rows // 2
    grad_key = jnp.zeros((rows, LANES), F32)
    grad_value = jnp.zeros((rows, LANES), F32)
    grad_query = []
    for low in range(0, rows, step):
        part = flow[low : low + step]
        weights = prob_ref[0, low : low + step, :]
        prob = weights.astype(F32)
        grad_prob = dot(part, value, 1, 1)
        delta = jnp.sum(grad_prob * prob, axis=-1, keepdims=True)
        grad_score = (prob * (grad_prob - delta)).astype(BF16)
        grad_query.append((dot(grad_score, key, 1, 0) * SCALE).astype(BF16))
        grad_key += dot(grad_score, query[low : low + step], 0, 0)
        grad_value += dot(weights, part, 0, 0)
    joined[head, :, :LANES] = jnp.concatenate(grad_query, axis=0)
    joined[head, :, LANES : 2 * LANES] = (grad_key * SCALE).astype(BF16)
    joined[head, :, 2 * LANES :] = grad_value.astype(BF16)

    if last:

        @pl.when(head == heads - 1)
        def _():
            fetch.wait()
            pieces = [earlier[index] for index in range(earlier.shape[0])]
            pieces += [joined[index] for index in range(heads)]
            everything = jnp.concatenate(pieces, axis=1)
            hand_out(dot(everything, mixing[...], 1, 0), keep0, keep2, send)


def backward(counts, grads, output_pad, packed, probs, first, heads, rest=()):
    rows_dev, width = grads[0].shape
    rows = rows_dev * MP
    wide = 3 * LANES
    block = full(rows_dev, width)
    stacked = pltpu.VMEM((rows, width), BF16)
    if rest:
        earlier, mixing_pad = rest
        out_shape = handed_shapes(rows_dev, width)
        more_specs = [full(*earlier.shape), HBM]
        out_specs = (block, block, full(2 * rows_dev, width))
        scratch = [
            stacked,
            pltpu.VMEM((heads, rows, wide), BF16),
            pltpu.VMEM(mixing_pad.shape, BF16),
            pltpu.SemaphoreType.DMA,
        ]
    else:
        out_shape = shape((heads, rows, wide), BF16)
        more_specs = []
        out_specs = full(heads, rows, wide)
        scratch = [stacked]
    return pl.pallas_call(
        partial(backward_kernel, heads, bool(rest), rows_dev),
        grid=(heads,),
        out_shape=out_shape,
        in_specs=[SMEM]
        + [block] * MP
        + [
            pl.BlockSpec((LANES, width), lambda head: (head + first, 0)),
            pl.BlockSpec((rows, wide), lambda head: (0, head + first)),
            pl.BlockSpec((1, rows, rows), lambda head: (head + first, 0, 0)),
        ]
        + more_specs,
        out_specs=out_specs,
        scratch_shapes=scratch,
        cost_estimate=cost(3e9, 6e6),
        name="backward_attention",
        compiler_params=grant(24),
    )(counts, *grads, output_pad, packed, probs, *rest)


def score_kernel(
    rows_dev, few, counts_ref, patch_ref, part_ref, near_ref, far_ref, embed_ref, tokens_ref,
    hidden_ref, best_ref, page_emb
):
    mine = lax.axis_index("dp")

    @pl.when(pl.program_id(0) == 0)
    def _():
        mixed = part_ref[...].astype(F32) + near_ref[...].astype(F32) + far_ref[...].astype(F32)
        hidden = (patch_ref[...].astype(F32) + mixed).astype(BF16)
        hidden_ref[...] = hidden
        embedded = dot(hidden, embed_ref[...], 1, 0)
        page_emb[...] = unit_rows(embedded).astype(BF16)

    similar = dot(page_emb[...], tokens_ref[...], 1, 1)
    lines = lax.broadcasted_iota(jnp.int32, (rows_dev, 1), 0) + lax.axis_index("mp") * rows_dev
    similar = jnp.where(lines < counts_ref[mine], similar, -2.0)
    best = jnp.max(similar, axis=0, keepdims=True)
    if few:
        size = best_ref.shape[1]
        for piece in range(best.shape[1] // size):
            row = best[:, piece * size : (piece + 1) * size]
            for copy in range(MP):
                best_ref[pl.ds((mine ^ piece) * MP + copy, 1), :] = row
    else:
        best_ref[...] = best


def hidden_and_best(counts, patches, part, received, far, embed_weight, tokens, few, local):
    rows_dev, width = patches.shape
    size = tokens.shape[0]
    chunk = size if few else math.gcd(size, 1024)
    block = full(rows_dev, width)
    if few:
        best_shape, best_spec = shape((size // local * MP, local), F32), full(size // local * MP, local)
    else:
        best_shape, best_spec = shape((1, size), F32), pl.BlockSpec((1, chunk), lambda index: (0, index))
    return pl.pallas_call(
        partial(score_kernel, rows_dev, few),
        grid=(size // chunk,),
        out_shape=(shape((rows_dev, width), BF16), best_shape),
        in_specs=[SMEM]
        + [block] * 4
        + [full(width, EMB), pl.BlockSpec((chunk, EMB), lambda index: (index, 0))],
        out_specs=(block, best_spec),
        scratch_shapes=[pltpu.VMEM((rows_dev, EMB), BF16)],
        cost_estimate=cost(1e8, 2e6),
        name="hidden_and_best",
        compiler_params=grant(12),
    )(counts, patches, part, received, far, embed_weight, tokens)


def page_score_kernel(found_ref, score_ref):
    pages = found_ref.shape[0] // MP
    best = jnp.max(found_ref[...].reshape(pages, MP, found_ref.shape[1]), axis=1)
    turned = best.T
    for query in range(score_ref.shape[0]):
        score_ref[query : query + 1, :] = jnp.sum(
            turned[query * QTOK : (query + 1) * QTOK], axis=0, keepdims=True
        )


def page_scores(found):
    return pl.pallas_call(
        page_score_kernel,
        out_shape=shape((found.shape[1] // QTOK, found.shape[0] // MP), F32),
        in_specs=[VMEM],
        out_specs=VMEM,
        name="page_scores",
        compiler_params=grant(4),
    )(found)


def norm_back_kernel(patch_ref, gain_ref, grad_ref, part_ref, near_ref, far_ref, out_ref):
    values = patch_ref[...].astype(F32)
    center = values - jnp.mean(values, axis=-1, keepdims=True)
    spread = jnp.mean(center * center, axis=-1, keepdims=True)
    inverse = lax.rsqrt(spread + 1e-06)
    flow = part_ref[...].astype(F32) + near_ref[...].astype(F32) + far_ref[...].astype(F32)
    flow = flow * gain_ref[...]
    along = jnp.mean(flow * center, axis=-1, keepdims=True)
    level = jnp.mean(flow, axis=-1, keepdims=True)
    result = inverse * (flow - level - center * (inverse * inverse * along))
    out_ref[...] = (grad_ref[...].astype(F32) + result).astype(BF16)


def norm_back(patches, gain, grads, part, near, far):
    block = full(*patches.shape)
    return pl.pallas_call(
        norm_back_kernel,
        grid=(1,),
        out_shape=shape(patches.shape, BF16),
        in_specs=[block, full(*gain.shape), block, block, block, block],
        out_specs=block,
        cost_estimate=cost(3e6, 2e6),
        name="norm_back",
        compiler_params=grant(12),
    )(patches, gain, grads, part, near, far)


def swap(values, axis, distance):
    size = lax.axis_size(axis)
    return lax.ppermute(values, axis, [(index, index ^ distance) for index in range(size)])


def scatter_sum(parts):
    part0, part2, send = parts
    received = swap(send, "mp", 1)
    relayed = received[part2.shape[0] :]
    far = swap((part2.astype(F32) + relayed.astype(F32)).astype(BF16), "mp", 2)
    return part0, received, far


def after(values, *others):
    return lax.optimization_barrier((values, *others))[0]


def body(
    patches,
    norm_gain,
    query_key_value,
    output_weight,
    embed_weight,
    query_tokens,
    patch_counts,
    positive_page,
    hidden_grad,
):
    data_index = lax.axis_index("dp")
    data_size = lax.axis_size("dp")
    few = data_size == 8
    heads = output_weight.shape[1] // HEAD_DIM
    gain = norm_gain.reshape(1, -1)

    rows2 = swap(patches, "mp", 2)
    rows1 = swap(patches, "mp", 1)
    grads2 = swap(hidden_grad, "mp", 2)
    grads1 = swap(hidden_grad, "mp", 1)

    local = query_tokens.shape[0]
    mixing_pad, output_pad, query_emb = prepare(
        query_key_value.T, output_weight.T, query_tokens.reshape(local * QTOK, EMB), heads
    )
    rows3 = swap(after(rows2, query_emb), "mp", 1)
    if few:
        tokens = query_emb
        for distance in (1, 2, 4):
            tokens = jnp.concatenate([tokens, swap(tokens, "dp", distance)], axis=0)
    else:
        tokens = lax.all_gather(query_emb, "dp", axis=0, tiled=True)

    packed, probs, attended, *parts = forward(
        patch_counts, (patches, rows1, rows2, rows3), gain, mixing_pad, output_pad, heads
    )
    grads3 = swap(after(grads2, rows3), "mp", 1)
    grads = (hidden_grad, grads1, grads2, grads3)
    part, received, far = scatter_sum(parts)
    half = heads // 2
    common = (patch_counts, grads, output_pad, packed, probs)
    if few:
        order = ((0, 4), (2, 6), (1, 5, 3, 7))
        kept, second, first = weight_parts(grads, after(attended, received), order)
        got1 = swap(first, "dp", 1).astype(F32)
        earlier = backward(*common[:4], after(probs, kept), 0, half)
        tokens = after(tokens, earlier)
    else:
        (whole,) = weight_parts(grads, attended, None)
        weight_grad = lax.psum_scatter(whole, "dp", scatter_dimension=0, tiled=True)
        earlier = backward(*common, 0, half)
    hidden, best = hidden_and_best(
        patch_counts, patches, part, received, far, embed_weight, tokens, few, local * QTOK
    )
    if few:
        middle = kept.shape[0]
        share = middle // 2
        going = (second.astype(F32) + got1[middle:]).astype(BF16)
        got2 = swap(going, "dp", 2).astype(F32)
        earlier = after(earlier, best, going)
    grad_parts = backward(*common, half, heads - half, (earlier, mixing_pad))
    part, received, far = scatter_sum(grad_parts)
    patch_grad = norm_back(patches, gain, hidden_grad, part, received, far)
    if few:
        kept = kept + got1[:middle] + got2
        weight_grad = kept[:share] + swap(kept[share:].astype(BF16), "dp", 4).astype(F32)
        my_scores = page_scores(lax.all_to_all(best, ("dp", "mp"), 0, 0, tiled=True))
    else:
        best = jnp.maximum(best, swap(best, "mp", 1))
        best = jnp.maximum(best, swap(best, "mp", 2))
        part_scores = jnp.sum(best.reshape(-1, QTOK), axis=1)
        every = lax.all_gather(part_scores.reshape(-1, 1), "dp", axis=1, tiled=True)
        my_scores = lax.dynamic_slice_in_dim(every, data_index * local, local, 0)
    columns = jnp.arange(my_scores.shape[1], dtype=jnp.int32)
    chosen = columns[None, :] == positive_page[:, None]
    positive_score = jnp.sum(jnp.where(chosen, my_scores, 0.0), axis=1)
    negative_score = jnp.max(jnp.where(chosen, -1e30, my_scores), axis=1)
    loss = jax.nn.softplus(negative_score - positive_score)
    return (hidden, patch_grad, weight_grad, my_scores, loss)


def solution(mesh):
    return jax.shard_map(
        body,
        mesh=mesh,
        in_specs=(
            P(("dp", "mp"), None),
            P(),
            P(None, "mp"),
            P(None, "mp"),
            P(),
            P("dp", None, None),
            P(),
            P("dp"),
            P(("dp", "mp"), None),
        ),
        out_specs=(
            P(("dp", "mp"), None),
            P(("dp", "mp"), None),
            P("dp", "mp"),
            P("dp", None),
            P("dp"),
        ),
        check_vma=False,
    )
```

```python
from functools import partial
import math

import jax
import jax.numpy as jnp
from jax import lax
from jax.experimental import pallas as pl
from jax.experimental.pallas import tpu as pltpu
from jax.sharding import PartitionSpec as P


HEAD_DIM = 72
LANES = 128
EMB = 128
QTOK = 32
MP = 4
HEAD_GROUP = 4
DISTANCES = (4, 1, 2)
ARRIVAL = (0, 4, 1, 5, 2, 6, 3, 7)
SCALE = HEAD_DIM ** (-0.5)
LOG2E = math.log2(math.e)
F32 = jnp.float32
BF16 = jnp.bfloat16

VMEM = pl.BlockSpec(memory_space=pltpu.VMEM)
SMEM = pl.BlockSpec(memory_space=pltpu.SMEM)
HBM = pl.BlockSpec(memory_space=pl.ANY)


def dot(left, right, left_dim, right_dim):
    return lax.dot_general(
        left, right, (((left_dim,), (right_dim,)), ((), ())), preferred_element_type=F32
    )


def shape(dims, kind):
    return jax.ShapeDtypeStruct(dims, kind)


def cost(flops, size, exps=0):
    return pl.CostEstimate(flops=int(flops), bytes_accessed=int(size), transcendentals=int(exps))


def grant(mebibytes):
    return pltpu.CompilerParams(vmem_limit_bytes=mebibytes * 1024 * 1024)


def full(*dims):
    return pl.BlockSpec(dims, lambda *_: (0,) * len(dims))


def unit_rows(values):
    return values * lax.rsqrt(jnp.sum(values * values, axis=-1, keepdims=True) + 1e-06)


def place_of(index, model_index, rows_dev):
    return (model_index ^ (index // rows_dev)) * rows_dev + index % rows_dev


def prepare_kernel(heads, mixing_ref, output_ref, tokens_ref, mixing_pad, output_pad, unit_ref):
    def spread(source, target, index):
        target[index * LANES : index * LANES + HEAD_DIM, :] = source[
            index * HEAD_DIM : (index + 1) * HEAD_DIM, :
        ]
        target[index * LANES + HEAD_DIM : (index + 1) * LANES, :] = jnp.zeros(
            (LANES - HEAD_DIM, target.shape[1]), BF16
        )

    values = tokens_ref[...].astype(F32)
    unit_ref[...] = unit_rows(values).astype(BF16)
    for index in range(3 * heads):
        spread(mixing_ref, mixing_pad, index)
    for index in range(heads):
        spread(output_ref, output_pad, index)


def prepare(mixing, output, tokens, heads):
    width = mixing.shape[1]
    return pl.pallas_call(
        partial(prepare_kernel, heads),
        out_shape=(
            shape((3 * heads * LANES, width), BF16),
            shape((heads * LANES, width), BF16),
            shape(tokens.shape, BF16),
        ),
        in_specs=[VMEM] * 3,
        out_specs=(VMEM,) * 3,
        cost_estimate=cost(0, 8e6),
        name="prepare",
        compiler_params=grant(24),
    )(mixing, output, tokens)


def hand_out(product, keep0, keep2, send):
    size = keep0.shape[0]
    keep0[...] = product[:size].astype(BF16)
    send[:size, :] = product[size : 2 * size].astype(BF16)
    keep2[...] = product[2 * size : 3 * size].astype(BF16)
    send[size:, :] = product[3 * size :].astype(BF16)


def forward_kernel(
    heads,
    rows_dev,
    counts_ref,
    rows0,
    rows1,
    rows2,
    rows3,
    gain_ref,
    mixing_ref,
    output_ref,
    packed_ref,
    prob_ref,
    attended_ref,
    keep0,
    keep2,
    send,
    normed,
):
    turn = pl.program_id(0)
    rows = rows_dev * MP
    group = prob_ref.shape[0]

    @pl.when(turn == 0)
    def _():
        for index, block in enumerate((rows0, rows1, rows2, rows3)):
            values = block[...].astype(F32)
            center = values - jnp.mean(values, axis=-1, keepdims=True)
            spread = jnp.mean(center * center, axis=-1, keepdims=True)
            normed[index * rows_dev : (index + 1) * rows_dev, :] = (
                center * lax.rsqrt(spread + 1e-06) * gain_ref[...]
            ).astype(BF16)

    packed = dot(normed[...], mixing_ref[...], 1, 1).astype(BF16)
    packed_ref[...] = packed
    count = counts_ref[lax.axis_index("dp")]
    model_index = lax.axis_index("mp")
    columns = lax.broadcasted_iota(jnp.int32, (1, rows), 1)
    seen = place_of(columns, model_index, rows_dev) < count
    lines = lax.broadcasted_iota(jnp.int32, (rows, 1), 0)
    live = place_of(lines, model_index, rows_dev) < count
    for index in range(group):
        own = packed[:, index * 3 * LANES : (index + 1) * 3 * LANES]
        query, key, value = own[:, :LANES], own[:, LANES : 2 * LANES], own[:, 2 * LANES :]
        score = dot(query, key, 1, 1)
        score = jnp.where(seen, score, -1e30)
        largest = jnp.max(score, axis=-1, keepdims=True)
        raised = jnp.exp2((score - largest) * (SCALE * LOG2E))
        total = jnp.sum(raised, axis=-1, keepdims=True)
        prob = (raised * (1.0 / total)).astype(BF16)
        prob_ref[index] = prob
        found = dot(prob, value, 1, 0)
        attended_ref[turn * group + index] = jnp.where(live, found, 0.0).astype(BF16)

    @pl.when(turn == pl.num_programs(0) - 1)
    def _():
        joined = jnp.concatenate([attended_ref[index] for index in range(heads)], axis=1)
        hand_out(dot(joined, output_ref[...], 1, 0), keep0, keep2, send)


def handed_shapes(rows_dev, width):
    kept = shape((rows_dev, width), BF16)
    return (kept, kept, shape((2 * rows_dev, width), BF16))


def forward(counts, blocks, gain, mixing_pad, output_pad, heads):
    rows_dev, width = blocks[0].shape
    rows = rows_dev * MP
    wide = 3 * LANES
    group = HEAD_GROUP if heads % HEAD_GROUP == 0 else 1
    block = full(rows_dev, width)
    return pl.pallas_call(
        partial(forward_kernel, heads, rows_dev),
        grid=(heads // group,),
        out_shape=(
            shape((rows, heads * wide), BF16),
            shape((heads, rows, rows), BF16),
            shape((heads, rows, LANES), BF16),
        )
        + handed_shapes(rows_dev, width),
        in_specs=[SMEM]
        + [block] * MP
        + [
            full(1, width),
            pl.BlockSpec((group * wide, width), lambda turn: (turn, 0)),
            full(heads * LANES, width),
        ],
        out_specs=(
            pl.BlockSpec((rows, group * wide), lambda turn: (0, turn)),
            pl.BlockSpec((group, rows, rows), lambda turn: (turn, 0, 0)),
            full(heads, rows, LANES),
        )
        + (block, block, full(2 * rows_dev, width)),
        scratch_shapes=[pltpu.VMEM((rows, width), BF16)],
        cost_estimate=cost(3e9, 12e6, heads * rows * rows),
        name="forward_attention",
        compiler_params=grant(28),
    )(counts, *blocks, gain, mixing_pad, output_pad)


def weight_kernel(
    heads, rows_dev, order, counts_ref, grad0, grad1, grad2, grad3, attended_ref, output_ref, *refs
):
    (flow_ref, *outs), (stacked, result) = refs[: len(refs) - 2], refs[len(refs) - 2 :]
    for index, block in enumerate((grad0, grad1, grad2, grad3)):
        stacked[index * rows_dev : (index + 1) * rows_dev, :] = block[...]
    joined = jnp.concatenate([attended_ref[index] for index in range(heads)], axis=1)
    count = counts_ref[lax.axis_index("dp")]
    lines = lax.broadcasted_iota(jnp.int32, (rows_dev * MP, 1), 0)
    live = place_of(lines, lax.axis_index("mp"), rows_dev) < count
    flow = dot(stacked[...], output_ref[...], 1, 1)
    flow_ref[...] = jnp.where(live, flow, 0.0).astype(BF16)
    product = dot(stacked[...], joined, 0, 0)
    for index in range(heads):
        result[:, index * HEAD_DIM : (index + 1) * HEAD_DIM] = product[
            :, index * LANES : index * LANES + HEAD_DIM
        ]
    if order is None:
        outs[0][...] = result[...]
    else:
        mine = lax.axis_index("dp")
        share = result.shape[0] // sum(len(group) for group in order)
        for group, out in zip(order, outs):
            for spot, piece in enumerate(group):
                start = pl.multiple_of((mine ^ piece) * share, 16)
                out[spot * share : (spot + 1) * share, :] = result[
                    pl.ds(start, share), :
                ].astype(out.dtype)


def weight_parts(counts, grads, attended, output_pad, order):
    rows_dev, width = grads[0].shape
    heads = attended.shape[0]
    narrow = heads * HEAD_DIM
    if order is None:
        outs = (shape((width, narrow), F32),)
    else:
        share = width // sum(len(group) for group in order)
        outs = tuple(
            shape((len(group) * share, narrow), F32 if index == 0 else BF16)
            for index, group in enumerate(order)
        )
    outs = (shape((rows_dev * MP, heads * LANES), BF16),) + outs
    return pl.pallas_call(
        partial(weight_kernel, heads, rows_dev, order),
        out_shape=outs,
        in_specs=[SMEM] + [VMEM] * (MP + 2),
        out_specs=(VMEM,) * len(outs),
        scratch_shapes=[
            pltpu.VMEM((rows_dev * MP, width), BF16),
            pltpu.VMEM((width, narrow), F32),
        ],
        cost_estimate=cost(7e8, 4e6),
        name="weight_parts",
        compiler_params=grant(20),
    )(counts, *grads, attended, output_pad)


def backward_kernel(last, flow_ref, packed_ref, prob_ref, *refs):
    if last:
        earlier, mixing_hbm, keep0, keep2, send, mixing, sem = refs
        fetch = pltpu.make_async_copy(mixing_hbm, mixing, sem)
        fetch.start()
    pieces = []
    for index in range(prob_ref.shape[0]):
        flow = flow_ref[:, index * LANES : (index + 1) * LANES]
        own = packed_ref[:, index * 3 * LANES : (index + 1) * 3 * LANES]
        query, key, value = own[:, :LANES], own[:, LANES : 2 * LANES], own[:, 2 * LANES :]
        weights = prob_ref[index]
        prob = weights.astype(F32)
        grad_prob = dot(flow, value, 1, 1)
        delta = jnp.sum(grad_prob * prob, axis=-1, keepdims=True)
        grad_score = (prob * (grad_prob - delta)).astype(BF16)
        pieces.append((dot(grad_score, key, 1, 0) * SCALE).astype(BF16))
        pieces.append((dot(grad_score, query, 0, 0) * SCALE).astype(BF16))
        pieces.append(dot(weights, flow, 0, 0).astype(BF16))
    if last:
        fetch.wait()
        everything = jnp.concatenate([earlier[...]] + pieces, axis=1)
        hand_out(dot(everything, mixing[...], 1, 0), keep0, keep2, send)
    else:
        for index, piece in enumerate(pieces):
            refs[0][:, index * LANES : (index + 1) * LANES] = piece


def backward(flow, packed, probs, first, heads, rest=()):
    rows = flow.shape[0]
    rows_dev = rows // MP
    wide = 3 * LANES
    if rest:
        earlier, mixing_pad = rest
        width = mixing_pad.shape[1]
        out_shape = handed_shapes(rows_dev, width)
        more_specs = [full(*earlier.shape), HBM]
        out_specs = (full(rows_dev, width), full(rows_dev, width), full(2 * rows_dev, width))
        scratch = [pltpu.VMEM(mixing_pad.shape, BF16), pltpu.SemaphoreType.DMA]
    else:
        out_shape = shape((rows, heads * wide), BF16)
        more_specs = []
        out_specs = full(rows, heads * wide)
        scratch = []
    turn = first // heads
    return pl.pallas_call(
        partial(backward_kernel, bool(rest)),
        grid=(1,),
        out_shape=out_shape,
        in_specs=[
            pl.BlockSpec((rows, heads * LANES), lambda _: (0, turn)),
            pl.BlockSpec((rows, heads * wide), lambda _: (0, turn)),
            pl.BlockSpec((heads, rows, rows), lambda _: (turn, 0, 0)),
        ]
        + more_specs,
        out_specs=out_specs,
        scratch_shapes=scratch,
        cost_estimate=cost(3e9, 6e6),
        name="backward_last" if rest else "backward_first",
        compiler_params=grant(28),
    )(flow, packed, probs, *rest)


def score_kernel(
    rows_dev, few, counts_ref, patch_ref, part_ref, near_ref, far_ref, embed_ref, tokens_ref,
    hidden_ref, best_ref, page_emb
):
    mine = lax.axis_index("dp")

    @pl.when(pl.program_id(0) == 0)
    def _():
        mixed = part_ref[...].astype(F32) + near_ref[...].astype(F32) + far_ref[...].astype(F32)
        hidden = (patch_ref[...].astype(F32) + mixed).astype(BF16)
        hidden_ref[...] = hidden
        embedded = dot(hidden, embed_ref[...], 1, 0)
        page_emb[...] = unit_rows(embedded).astype(BF16)

    similar = dot(page_emb[...], tokens_ref[...], 1, 1)
    lines = lax.broadcasted_iota(jnp.int32, (rows_dev, 1), 0) + lax.axis_index("mp") * rows_dev
    similar = jnp.where(lines < counts_ref[mine], similar, -2.0)
    best = jnp.max(similar, axis=0, keepdims=True)
    if few:
        size = best_ref.shape[1]
        for piece in range(best.shape[1] // size):
            row = best[:, piece * size : (piece + 1) * size]
            for copy in range(MP):
                best_ref[pl.ds((mine ^ ARRIVAL[piece]) * MP + copy, 1), :] = row
    else:
        best_ref[...] = best


def hidden_and_best(counts, patches, part, received, far, embed_weight, tokens, few, local):
    rows_dev, width = patches.shape
    size = tokens.shape[0]
    chunk = size if few else math.gcd(size, 1024)
    block = full(rows_dev, width)
    if few:
        best_shape, best_spec = shape((size // local * MP, local), F32), full(size // local * MP, local)
    else:
        best_shape, best_spec = shape((1, size), F32), pl.BlockSpec((1, chunk), lambda index: (0, index))
    return pl.pallas_call(
        partial(score_kernel, rows_dev, few),
        grid=(size // chunk,),
        out_shape=(shape((rows_dev, width), BF16), best_shape),
        in_specs=[SMEM]
        + [block] * 4
        + [full(width, EMB), pl.BlockSpec((chunk, EMB), lambda index: (index, 0))],
        out_specs=(block, best_spec),
        scratch_shapes=[pltpu.VMEM((rows_dev, EMB), BF16)],
        cost_estimate=cost(1e8, 2e6),
        name="hidden_and_best",
        compiler_params=grant(12),
    )(counts, patches, part, received, far, embed_weight, tokens)


def norm_back_kernel(patch_ref, gain_ref, grad_ref, part_ref, near_ref, far_ref, *refs):
    values = patch_ref[...].astype(F32)
    center = values - jnp.mean(values, axis=-1, keepdims=True)
    spread = jnp.mean(center * center, axis=-1, keepdims=True)
    inverse = lax.rsqrt(spread + 1e-06)
    flow = part_ref[...].astype(F32) + near_ref[...].astype(F32) + far_ref[...].astype(F32)
    flow = flow * gain_ref[...]
    along = jnp.mean(flow * center, axis=-1, keepdims=True)
    level = jnp.mean(flow, axis=-1, keepdims=True)
    result = inverse * (flow - level - center * (inverse * inverse * along))
    out = (grad_ref[...].astype(F32) + result).astype(BF16)
    if len(refs) == 1:
        refs[0][...] = out
        return
    mine_ref, other_ref, found_ref, positive_ref, out_ref, weight_ref, score_ref, loss_ref = refs
    out_ref[...] = out
    weight_ref[...] = mine_ref[...] + other_ref[...].astype(F32)
    pages = found_ref.shape[0] // MP
    best = jnp.max(found_ref[...].reshape(pages, MP, found_ref.shape[1]), axis=1)
    turned = best.T
    columns = lax.broadcasted_iota(jnp.int32, (1, pages), 1)
    for query in range(score_ref.shape[0]):
        row = jnp.sum(turned[query * QTOK : (query + 1) * QTOK], axis=0, keepdims=True)
        score_ref[query : query + 1, :] = row
        chosen = columns == positive_ref[query]
        positive = jnp.sum(jnp.where(chosen, row, 0.0), axis=1, keepdims=True)
        negative = jnp.max(jnp.where(chosen, -1e30, row), axis=1, keepdims=True)
        gap = negative - positive
        loss = jnp.maximum(gap, 0.0) + jnp.log1p(jnp.exp(-jnp.abs(gap)))
        loss_ref[query] = loss[0, 0]


def norm_back(patches, gain, grads, part, near, far, more=()):
    block = full(*patches.shape)
    out_shape, out_specs, specs = [shape(patches.shape, BF16)], [block], []
    if more:
        mine, _, found, positive = more
        scores = (positive.shape[0], found.shape[0] // MP)
        specs = [full(*mine.shape), full(*mine.shape), full(*found.shape), SMEM]
        out_shape += [shape(mine.shape, F32), shape(scores, F32), shape(positive.shape, F32)]
        out_specs += [full(*mine.shape), full(*scores), SMEM]
    return pl.pallas_call(
        norm_back_kernel,
        grid=(1,),
        out_shape=tuple(out_shape),
        in_specs=[block, full(*gain.shape), block, block, block, block] + specs,
        out_specs=tuple(out_specs),
        cost_estimate=cost(3e6, 2e6),
        name="norm_back",
        compiler_params=grant(12),
    )(patches, gain, grads, part, near, far, *more)


def join_kernel(kept_ref, got1_ref, got2_ref, mine_ref, send_ref):
    half, share = kept_ref.shape[0], mine_ref.shape[0]
    total = kept_ref[...] + got1_ref[:half, :].astype(F32) + got2_ref[...].astype(F32)
    mine_ref[...] = total[:share]
    send_ref[...] = total[share:].astype(BF16)


def join_parts(kept, got1, got2):
    share = (kept.shape[0] // 2, kept.shape[1])
    return pl.pallas_call(
        join_kernel,
        out_shape=(shape(share, F32), shape(share, BF16)),
        in_specs=[VMEM] * 3,
        out_specs=(VMEM,) * 2,
        cost_estimate=cost(3e5, 1e6),
        name="join_parts",
        compiler_params=grant(6),
    )(kept, got1, got2)


def swap(values, axis, distance):
    size = lax.axis_size(axis)
    return lax.ppermute(values, axis, [(index, index ^ distance) for index in range(size)])


def scatter_sum(parts):
    part0, part2, send = parts
    received = swap(send, "mp", 1)
    relayed = received[part2.shape[0] :]
    going = (part2.astype(F32) + relayed.astype(F32)).astype(BF16)
    return part0, received, swap(going, "mp", 2), going


def after(values, *others):
    return lax.optimization_barrier((values, *others))[0]


def body(
    patches,
    norm_gain,
    query_key_value,
    output_weight,
    embed_weight,
    query_tokens,
    patch_counts,
    positive_page,
    hidden_grad,
):
    data_index = lax.axis_index("dp")
    data_size = lax.axis_size("dp")
    few = data_size == 8
    heads = output_weight.shape[1] // HEAD_DIM
    gain = norm_gain.reshape(1, -1)

    rows2 = swap(patches, "mp", 2)
    rows1 = swap(patches, "mp", 1)
    grads2 = swap(hidden_grad, "mp", 2)
    grads1 = swap(hidden_grad, "mp", 1)

    local = query_tokens.shape[0]
    mixing_pad, output_pad, query_emb = prepare(
        query_key_value.T, output_weight.T, query_tokens.reshape(local * QTOK, EMB), heads
    )
    if few:
        tokens = query_emb
        for distance in DISTANCES[:2]:
            other = swap(tokens, "dp", distance)
            tokens = jnp.concatenate([tokens, other], axis=0)
    else:
        tokens = lax.all_gather(query_emb, "dp", axis=0, tiled=True)
    rows2 = after(rows2, query_emb)
    rows3 = swap(rows2, "mp", 1)

    packed, probs, attended, *parts = forward(
        patch_counts, (patches, rows1, rows2, rows3), gain, mixing_pad, output_pad, heads
    )
    grads3 = swap(after(grads2, rows3), "mp", 1)
    grads = (hidden_grad, grads1, grads2, grads3)
    part, received, far, _ = scatter_sum(parts)
    half = heads - heads // 4
    if few:
        order = ((0, 4), (2, 6), (1, 5, 3, 7))
        flow, kept, second, first = weight_parts(patch_counts, grads, attended, output_pad, order)
        got1 = swap(first, "dp", 1)
        other = swap(tokens, "dp", 2)
        tokens = jnp.concatenate([tokens, after(other, kept)], axis=0)
        earlier = backward(flow, packed, probs, 0, half)
        tokens = after(tokens, earlier)
    else:
        flow, whole = weight_parts(patch_counts, grads, attended, output_pad, None)
        weight_grad = lax.psum_scatter(whole, "dp", scatter_dimension=0, tiled=True)
        earlier = backward(flow, packed, probs, 0, half)
    hidden, best = hidden_and_best(
        patch_counts, patches, part, received, far, embed_weight, tokens, few, local * QTOK
    )
    if few:
        earlier, best = lax.optimization_barrier((earlier, best))
    grad_parts = backward(flow, packed, probs, half, heads - half, (earlier, mixing_pad))
    part, received, far, sent = scatter_sum(grad_parts)
    more = ()
    if few:
        going = (second.astype(F32) + got1[kept.shape[0] :].astype(F32)).astype(BF16)
        got2 = swap(going, "dp", 2)
        mine, send = join_parts(kept, got1, got2)
        other = swap(send, "dp", 4)
        found = lax.all_to_all(after(best, sent), ("dp", "mp"), 0, 0, tiled=True)
        more = (mine, other, found, positive_page)
    patch_grad, *rest = norm_back(patches, gain, hidden_grad, part, received, far, more)
    if few:
        return (hidden, patch_grad, *rest)
    best = jnp.maximum(best, swap(best, "mp", 1))
    best = jnp.maximum(best, swap(best, "mp", 2))
    part_scores = jnp.sum(best.reshape(-1, QTOK), axis=1)
    every = lax.all_gather(part_scores.reshape(-1, 1), "dp", axis=1, tiled=True)
    my_scores = lax.dynamic_slice_in_dim(every, data_index * local, local, 0)
    columns = jnp.arange(my_scores.shape[1], dtype=jnp.int32)
    chosen = columns[None, :] == positive_page[:, None]
    positive_score = jnp.sum(jnp.where(chosen, my_scores, 0.0), axis=1)
    negative_score = jnp.max(jnp.where(chosen, -1e30, my_scores), axis=1)
    loss = jax.nn.softplus(negative_score - positive_score)
    return (hidden, patch_grad, weight_grad, my_scores, loss)


def solution(mesh):
    return jax.shard_map(
        body,
        mesh=mesh,
        in_specs=(
            P(("dp", "mp"), None),
            P(),
            P(None, "mp"),
            P(None, "mp"),
            P(),
            P("dp", None, None),
            P(),
            P("dp"),
            P(("dp", "mp"), None),
        ),
        out_specs=(
            P(("dp", "mp"), None),
            P(("dp", "mp"), None),
            P("dp", "mp"),
            P("dp", None),
            P("dp"),
        ),
        check_vma=False,
    )
```

```python
from functools import partial
import math

import jax
import jax.numpy as jnp
from jax import lax
from jax.experimental import pallas as pl
from jax.experimental.pallas import tpu as pltpu
from jax.sharding import PartitionSpec as P


HEAD_DIM = 72
LANES = 128
HEAD_LANES = 256
EMB = 128
QTOK = 32
MP = 4
DISTANCES = (4, 1, 2)
ARRIVAL = (0, 4, 1, 5, 2, 6, 3, 7)
SCALE = HEAD_DIM ** (-0.5)
LOG2E = math.log2(math.e)
F32 = jnp.float32
BF16 = jnp.bfloat16

HBM = pl.BlockSpec(memory_space=pltpu.HBM)
VMEM = pl.BlockSpec(memory_space=pltpu.VMEM)
SMEM = pl.BlockSpec(memory_space=pltpu.SMEM)


def dot(left, right, left_dim, right_dim):
    return lax.dot_general(
        left, right, (((left_dim,), (right_dim,)), ((), ())), preferred_element_type=F32
    )


def shape(dims, kind):
    return jax.ShapeDtypeStruct(dims, kind)


def cost(flops, size, exps=0):
    return pl.CostEstimate(flops=int(flops), bytes_accessed=int(size), transcendentals=int(exps))


def grant(mebibytes):
    return pltpu.CompilerParams(vmem_limit_bytes=mebibytes * 1024 * 1024)


def full(*dims):
    return pl.BlockSpec(dims, lambda *_: (0,) * len(dims))


def unit_rows(values):
    return values * lax.rsqrt(jnp.sum(values * values, axis=-1, keepdims=True) + 1e-06)


def place_of(index, model_index, rows_dev):
    return (model_index ^ (index // rows_dev)) * rows_dev + index % rows_dev


def gain_row(gain_ref):
    return jnp.concatenate([gain_ref[row : row + 1, :] for row in range(gain_ref.shape[0])], axis=1)


def norm_rows(block, gain):
    values = block.astype(F32)
    center = values - jnp.mean(values, axis=-1, keepdims=True)
    spread = jnp.mean(center * center, axis=-1, keepdims=True)
    return (center * lax.rsqrt(spread + 1e-06) * gain).astype(BF16)


def prepare_kernel(
    heads, rows_hbm, gain_hbm, mixing_hbm, output_hbm, rows1, mixing_pad, output_pad, packed_ref,
    rows0, gain_ref, mixing_ref, output_ref, normed, sems
):
    def spread(source, target, index, size, room):
        target[index * room : index * room + size, :] = source[index * size : (index + 1) * size, :]
        target[index * room + size : (index + 1) * room, :] = jnp.zeros(
            (room - size, target.shape[1]), BF16
        )

    sources = (rows_hbm, gain_hbm, mixing_hbm, output_hbm)
    targets = (rows0, gain_ref, mixing_ref, output_ref)
    fetches = [
        pltpu.make_async_copy(source, target, sems.at[index])
        for index, (source, target) in enumerate(zip(sources, targets))
    ]
    for fetch in fetches:
        fetch.start()
    fetches[0].wait()
    fetches[1].wait()
    size = rows0.shape[0]
    gain = gain_row(gain_ref)
    for index, block in enumerate((rows0, rows1)):
        normed[index * size : (index + 1) * size, :] = norm_rows(block[...], gain)
    fetches[2].wait()
    for index in range(heads):
        spread(mixing_ref, mixing_pad, index, 3 * HEAD_DIM, HEAD_LANES)
    fetches[3].wait()
    for index in range(heads):
        spread(output_ref, output_pad, index, HEAD_DIM, LANES)
    packed_ref[...] = dot(normed[...], mixing_pad[...], 1, 1).astype(BF16)


def in_hbm(values):
    return pltpu.with_memory_space_constraint(values, pltpu.HBM)


def prepare(mixing, output, rows0, rows1, gain, heads):
    width = mixing.shape[1]
    size = 2 * rows0.shape[0]
    return pl.pallas_call(
        partial(prepare_kernel, heads),
        out_shape=(
            shape((heads * HEAD_LANES, width), BF16),
            shape((heads * LANES, width), BF16),
            shape((size, heads * HEAD_LANES), BF16),
        ),
        in_specs=[HBM] * 4 + [VMEM],
        out_specs=(VMEM,) * 3,
        scratch_shapes=[
            pltpu.VMEM(rows0.shape, BF16),
            pltpu.VMEM(gain.shape, F32),
            pltpu.VMEM(mixing.shape, BF16),
            pltpu.VMEM(output.shape, BF16),
            pltpu.VMEM((size, width), BF16),
            pltpu.SemaphoreType.DMA((4,)),
        ],
        cost_estimate=cost(1e9, 8e6),
        name="prepare",
        compiler_params=grant(24),
    )(in_hbm(rows0), in_hbm(gain), in_hbm(mixing), in_hbm(output), rows1)


def head_parts(packed_ref, head):
    start = head * HEAD_LANES
    ends = [start + index * HEAD_DIM for index in range(4)]
    return [packed_ref[:, low:high] for low, high in zip(ends, ends[1:])]


def hand_out(product, keep0, keep2, send):
    size = keep0.shape[0]
    keep0[...] = product[:size].astype(BF16)
    send[:size, :] = product[size : 2 * size].astype(BF16)
    keep2[...] = product[2 * size : 3 * size].astype(BF16)
    send[size:, :] = product[3 * size :].astype(BF16)


def forward_kernel(
    heads,
    rows_dev,
    counts_ref,
    early_ref,
    rows2,
    rows3,
    gain_ref,
    mixing_ref,
    output_ref,
    packed_ref,
    prob_ref,
    attended_ref,
    keep0,
    keep2,
    send,
    normed,
):
    rows = rows_dev * MP
    gain = gain_row(gain_ref)
    for index, block in enumerate((rows2, rows3)):
        normed[index * rows_dev : (index + 1) * rows_dev, :] = norm_rows(block[...], gain)
    half = 2 * rows_dev
    packed_ref[:half, :] = early_ref[...]
    packed_ref[half:, :] = dot(normed[...], mixing_ref[...], 1, 1).astype(BF16)
    count = counts_ref[lax.axis_index("dp")]
    model_index = lax.axis_index("mp")
    columns = lax.broadcasted_iota(jnp.int32, (1, rows), 1)
    seen = place_of(columns, model_index, rows_dev) < count
    lines = lax.broadcasted_iota(jnp.int32, (rows, 1), 0)
    live = place_of(lines, model_index, rows_dev) < count
    for head in range(heads):
        query, key, value = head_parts(packed_ref, head)
        score = dot(query, key, 1, 1)
        score = jnp.where(seen, score, -1e30)
        largest = jnp.max(score, axis=-1, keepdims=True)
        raised = jnp.exp2((score - largest) * (SCALE * LOG2E))
        total = jnp.sum(raised, axis=-1, keepdims=True)
        prob = (raised * (1.0 / total)).astype(BF16)
        prob_ref[head] = prob
        found = dot(prob, value, 1, 0)
        start = head * LANES
        attended_ref[:, start : start + HEAD_DIM] = jnp.where(live, found, 0.0).astype(BF16)
        attended_ref[:, start + HEAD_DIM : start + LANES] = jnp.zeros(
            (rows, LANES - HEAD_DIM), BF16
        )
    hand_out(dot(attended_ref[...], output_ref[...], 1, 0), keep0, keep2, send)


def handed_shapes(rows_dev, width):
    kept = shape((rows_dev, width), BF16)
    return (kept, kept, shape((2 * rows_dev, width), BF16))


def forward(counts, early, blocks, gain, mixing_pad, output_pad, heads):
    rows_dev, width = blocks[0].shape
    rows = rows_dev * MP
    return pl.pallas_call(
        partial(forward_kernel, heads, rows_dev),
        out_shape=(
            shape((rows, heads * HEAD_LANES), BF16),
            shape((heads, rows, rows), BF16),
            shape((rows, heads * LANES), BF16),
        )
        + handed_shapes(rows_dev, width),
        in_specs=[SMEM] + [VMEM] * 6,
        out_specs=(VMEM,) * 6,
        scratch_shapes=[pltpu.VMEM((2 * rows_dev, width), BF16)],
        cost_estimate=cost(3e9, 12e6, heads * rows * rows),
        name="forward_attention",
        compiler_params=grant(28),
    )(counts, early, *blocks, gain, mixing_pad, output_pad)


def weight_kernel(
    heads, rows_dev, order, grad0, grad1, grad2, grad3, attended_ref, *refs
):
    (stacked, *outs), (result,) = refs[: len(refs) - 1], refs[len(refs) - 1 :]
    for index, block in enumerate((grad0, grad1, grad2, grad3)):
        stacked[index * rows_dev : (index + 1) * rows_dev, :] = block[...]
    product = dot(stacked[...], attended_ref[...], 0, 0)
    for index in range(heads):
        result[:, index * HEAD_DIM : (index + 1) * HEAD_DIM] = product[
            :, index * LANES : index * LANES + HEAD_DIM
        ]
    if order is None:
        outs[0][...] = result[...]
    else:
        mine = lax.axis_index("dp")
        share = result.shape[0] // sum(len(group) for group in order)
        for group, out in zip(order, outs):
            for spot, piece in enumerate(group):
                start = pl.multiple_of((mine ^ piece) * share, 16)
                out[spot * share : (spot + 1) * share, :] = result[
                    pl.ds(start, share), :
                ].astype(out.dtype)


def weight_parts(grads, attended, order):
    rows_dev, width = grads[0].shape
    heads = attended.shape[1] // LANES
    narrow = heads * HEAD_DIM
    if order is None:
        outs = (shape((width, narrow), F32),)
    else:
        share = width // sum(len(group) for group in order)
        outs = tuple(
            shape((len(group) * share, narrow), F32 if index == 0 else BF16)
            for index, group in enumerate(order)
        )
    outs = (shape((rows_dev * MP, width), BF16),) + outs
    return pl.pallas_call(
        partial(weight_kernel, heads, rows_dev, order),
        out_shape=outs,
        in_specs=[VMEM] * (MP + 1),
        out_specs=(VMEM,) * len(outs),
        scratch_shapes=[pltpu.VMEM((width, narrow), F32)],
        cost_estimate=cost(7e8, 4e6),
        name="weight_parts",
        compiler_params=grant(20),
    )(*grads, attended)


def backward_kernel(heads, counts_ref, stacked_ref, output_ref, packed_ref, prob_ref, out_ref):
    rows = stacked_ref.shape[0]
    count = counts_ref[lax.axis_index("dp")]
    lines = lax.broadcasted_iota(jnp.int32, (rows, 1), 0)
    live = place_of(lines, lax.axis_index("mp"), rows // MP) < count
    flows = dot(stacked_ref[...], output_ref[...], 1, 1)
    flows = jnp.where(live, flows, 0.0).astype(BF16)
    for head in range(heads):
        flow = flows[:, head * LANES : head * LANES + HEAD_DIM]
        query, key, value = head_parts(packed_ref, head)
        weights = prob_ref[head]
        prob = weights.astype(F32)
        grad_prob = dot(flow, value, 1, 1)
        delta = jnp.sum(grad_prob * prob, axis=-1, keepdims=True)
        grad_score = (prob * (grad_prob - delta)).astype(BF16)
        parts = (
            (dot(grad_score, key, 1, 0) * SCALE).astype(BF16),
            (dot(grad_score, query, 0, 0) * SCALE).astype(BF16),
            dot(weights, flow, 0, 0).astype(BF16),
            jnp.zeros((rows, HEAD_LANES - 3 * HEAD_DIM), BF16),
        )
        out_ref[:, head * HEAD_LANES : (head + 1) * HEAD_LANES] = jnp.concatenate(parts, axis=1)


def backward(counts, stacked, output_pad, packed, probs):
    heads, rows, _ = probs.shape
    return pl.pallas_call(
        partial(backward_kernel, heads),
        out_shape=shape((rows, heads * HEAD_LANES), BF16),
        in_specs=[SMEM] + [VMEM] * 4,
        out_specs=VMEM,
        cost_estimate=cost(4e9, 6e6),
        name="backward_attention",
        compiler_params=grant(28),
    )(counts, stacked, output_pad, packed, probs)


def branch_kernel(joined_ref, mixing_ref, keep0, keep2, send):
    hand_out(dot(joined_ref[...], mixing_ref[...], 1, 0), keep0, keep2, send)


def input_branch(joined, mixing_pad):
    return pl.pallas_call(
        branch_kernel,
        out_shape=handed_shapes(joined.shape[0] // MP, mixing_pad.shape[1]),
        in_specs=[VMEM] * 2,
        out_specs=(VMEM,) * 3,
        cost_estimate=cost(2e9, 8e6),
        name="input_branch",
        compiler_params=grant(24),
    )(joined, mixing_pad)


def score_kernel(
    rows_dev, few, counts_ref, patch_ref, part_ref, near_ref, far_ref, embed_ref, tokens_ref,
    hidden_ref, best_ref, page_emb
):
    mine = lax.axis_index("dp")

    def embed():
        near = near_ref[: part_ref.shape[0], :]
        mixed = part_ref[...].astype(F32) + near.astype(F32) + far_ref[...].astype(F32)
        hidden = (patch_ref[...].astype(F32) + mixed).astype(BF16)
        hidden_ref[...] = hidden
        embedded = dot(hidden, embed_ref[...], 1, 0)
        page_emb[...] = unit_rows(embedded).astype(BF16)

    if few:
        embed()
    else:
        pl.when(pl.program_id(0) == 0)(embed)
    tokens = unit_rows(tokens_ref[...].astype(F32)).astype(BF16)
    similar = dot(page_emb[...], tokens, 1, 1)
    lines = lax.broadcasted_iota(jnp.int32, (rows_dev, 1), 0) + lax.axis_index("mp") * rows_dev
    similar = jnp.where(lines < counts_ref[mine], similar, -2.0)
    best = jnp.max(similar, axis=0, keepdims=True)
    if few:
        size = best_ref.shape[1]
        for piece in range(best.shape[1] // size):
            row = best[:, piece * size : (piece + 1) * size]
            for copy in range(MP):
                best_ref[pl.ds((mine ^ ARRIVAL[piece]) * MP + copy, 1), :] = row
    else:
        best_ref[...] = best


def hidden_and_best(counts, patches, part, received, far, embed_weight, tokens, few, local):
    rows_dev, width = patches.shape
    size = tokens.shape[0]
    chunk = size if few else math.gcd(size, 1024)
    block = full(rows_dev, width)
    if few:
        best_shape = shape((size // local * MP, local), F32)
        layout = dict(in_specs=[SMEM] + [VMEM] * 6, out_specs=(VMEM, VMEM))
    else:
        best_shape = shape((1, size), F32)
        layout = dict(
            grid=(size // chunk,),
            in_specs=[SMEM]
            + [block] * 4
            + [full(width, EMB), pl.BlockSpec((chunk, EMB), lambda index: (index, 0))],
            out_specs=(block, pl.BlockSpec((1, chunk), lambda index: (0, index))),
        )
    return pl.pallas_call(
        partial(score_kernel, rows_dev, few),
        **layout,
        out_shape=(shape((rows_dev, width), BF16), best_shape),
        scratch_shapes=[pltpu.VMEM((rows_dev, EMB), BF16)],
        cost_estimate=cost(1e8, 2e6),
        name="hidden_and_best",
        compiler_params=grant(12),
    )(counts, patches, part, received, far, embed_weight, tokens)


def norm_back_kernel(patch_ref, gain_ref, grad_ref, part_ref, near_ref, far_ref, *refs):
    values = patch_ref[...].astype(F32)
    center = values - jnp.mean(values, axis=-1, keepdims=True)
    spread = jnp.mean(center * center, axis=-1, keepdims=True)
    inverse = lax.rsqrt(spread + 1e-06)
    near = near_ref[: part_ref.shape[0], :]
    flow = part_ref[...].astype(F32) + near.astype(F32) + far_ref[...].astype(F32)
    flow = flow * gain_row(gain_ref)
    along = jnp.mean(flow * center, axis=-1, keepdims=True)
    level = jnp.mean(flow, axis=-1, keepdims=True)
    result = inverse * (flow - level - center * (inverse * inverse * along))
    out = (grad_ref[...].astype(F32) + result).astype(BF16)
    if len(refs) == 1:
        refs[0][...] = out
        return
    mine_ref, other_ref, found_ref, positive_ref, out_ref, weight_ref, score_ref, loss_ref = refs
    out_ref[...] = out
    weight_ref[...] = mine_ref[...] + other_ref[...].astype(F32)
    pages = found_ref.shape[0] // MP
    best = jnp.max(found_ref[...].reshape(pages, MP, found_ref.shape[1]), axis=1)
    turned = best.T
    columns = lax.broadcasted_iota(jnp.int32, (1, pages), 1)
    for query in range(score_ref.shape[0]):
        row = jnp.sum(turned[query * QTOK : (query + 1) * QTOK], axis=0, keepdims=True)
        score_ref[query : query + 1, :] = row
        chosen = columns == positive_ref[query]
        positive = jnp.sum(jnp.where(chosen, row, 0.0), axis=1, keepdims=True)
        negative = jnp.max(jnp.where(chosen, -1e30, row), axis=1, keepdims=True)
        gap = negative - positive
        loss = jnp.maximum(gap, 0.0) + jnp.log1p(jnp.exp(-jnp.abs(gap)))
        loss_ref[query] = loss[0, 0]


def norm_back(patches, gain, grads, part, near, far, more=()):
    out_shape, out_specs, specs = [shape(patches.shape, BF16)], [VMEM], []
    if more:
        mine, _, found, positive = more
        scores = (positive.shape[0], found.shape[0] // MP)
        specs = [VMEM, VMEM, VMEM, SMEM]
        out_shape += [shape(mine.shape, F32), shape(scores, F32), shape(positive.shape, F32)]
        out_specs += [VMEM, VMEM, SMEM]
    return pl.pallas_call(
        norm_back_kernel,
        out_shape=tuple(out_shape),
        in_specs=[VMEM] * 6 + specs,
        out_specs=tuple(out_specs),
        cost_estimate=cost(3e6, 2e6),
        name="norm_back",
        compiler_params=grant(12),
    )(patches, gain, grads, part, near, far, *more)


def join_kernel(kept_ref, got1_ref, got2_ref, mine_ref, send_ref):
    half, share = kept_ref.shape[0], mine_ref.shape[0]
    total = kept_ref[...] + got1_ref[:half, :].astype(F32) + got2_ref[...].astype(F32)
    mine_ref[...] = total[:share]
    send_ref[...] = total[share:].astype(BF16)


def join_parts(kept, got1, got2):
    share = (kept.shape[0] // 2, kept.shape[1])
    return pl.pallas_call(
        join_kernel,
        out_shape=(shape(share, F32), shape(share, BF16)),
        in_specs=[VMEM] * 3,
        out_specs=(VMEM,) * 2,
        cost_estimate=cost(3e5, 1e6),
        name="join_parts",
        compiler_params=grant(6),
    )(kept, got1, got2)


def swap(values, axis, distance):
    size = lax.axis_size(axis)
    return lax.ppermute(values, axis, [(index, index ^ distance) for index in range(size)])


def scatter_sum(parts):
    part0, part2, send = parts
    received = swap(send, "mp", 1)
    relayed = received[part2.shape[0] :]
    going = (part2.astype(F32) + relayed.astype(F32)).astype(BF16)
    return part0, received, swap(going, "mp", 2), going


def after(values, *others):
    return lax.optimization_barrier((values, *others))[0]


def body(
    patches,
    norm_gain,
    query_key_value,
    output_weight,
    embed_weight,
    query_tokens,
    patch_counts,
    positive_page,
    hidden_grad,
):
    data_index = lax.axis_index("dp")
    data_size = lax.axis_size("dp")
    few = data_size == 8
    heads = output_weight.shape[1] // HEAD_DIM
    gain = norm_gain.reshape(-1, LANES)

    rows2 = swap(patches, "mp", 2)
    rows1 = swap(patches, "mp", 1)
    grads2 = swap(hidden_grad, "mp", 2)
    grads1 = swap(hidden_grad, "mp", 1)

    local = query_tokens.shape[0]
    own_tokens = query_tokens.reshape(local * QTOK, EMB)
    mixing_pad, output_pad, early = prepare(
        query_key_value.T, output_weight.T, patches, rows1, gain, heads
    )
    if few:
        tokens = own_tokens
        for distance in DISTANCES[:2]:
            other = swap(tokens, "dp", distance)
            tokens = jnp.concatenate([tokens, other], axis=0)
    else:
        tokens = lax.all_gather(own_tokens, "dp", axis=0, tiled=True)
    rows2 = after(rows2, early)
    rows3 = swap(rows2, "mp", 1)

    packed, probs, attended, *parts = forward(
        patch_counts, early, (rows2, rows3), gain, mixing_pad, output_pad, heads
    )
    grads3 = swap(after(grads2, rows3), "mp", 1)
    grads = (hidden_grad, grads1, grads2, grads3)
    part, received, far, _ = scatter_sum(parts)
    if few:
        order = ((0, 4), (2, 6), (1, 5, 3, 7))
        stacked, kept, second, first = weight_parts(grads, attended, order)
        got1 = swap(first, "dp", 1)
        other = swap(tokens, "dp", 2)
        near_tokens = tokens
        joined = backward(patch_counts, stacked, output_pad, packed, probs)
        tokens = jnp.concatenate([after(near_tokens, joined), after(other, joined)], axis=0)
    else:
        stacked, whole = weight_parts(grads, attended, None)
        weight_grad = lax.psum_scatter(whole, "dp", scatter_dimension=0, tiled=True)
        joined = backward(patch_counts, stacked, output_pad, packed, probs)
    hidden, best = hidden_and_best(
        patch_counts, patches, part, received, far, embed_weight, tokens, few, local * QTOK
    )
    if few:
        joined, best = lax.optimization_barrier((joined, best))
    grad_parts = input_branch(joined, mixing_pad)
    part, received, far, sent = scatter_sum(grad_parts)
    more = ()
    if few:
        going = (second.astype(F32) + got1[kept.shape[0] :].astype(F32)).astype(BF16)
        got2 = swap(going, "dp", 2)
        mine, send = join_parts(kept, got1, got2)
        other = swap(send, "dp", 4)
        found = lax.all_to_all(after(best, sent), ("dp", "mp"), 0, 0, tiled=True)
        more = (mine, other, found, positive_page)
    patch_grad, *rest = norm_back(patches, gain, hidden_grad, part, received, far, more)
    if few:
        return (hidden, patch_grad, *rest)
    best = jnp.maximum(best, swap(best, "mp", 1))
    best = jnp.maximum(best, swap(best, "mp", 2))
    part_scores = jnp.sum(best.reshape(-1, QTOK), axis=1)
    every = lax.all_gather(part_scores.reshape(-1, 1), "dp", axis=1, tiled=True)
    my_scores = lax.dynamic_slice_in_dim(every, data_index * local, local, 0)
    columns = jnp.arange(my_scores.shape[1], dtype=jnp.int32)
    chosen = columns[None, :] == positive_page[:, None]
    positive_score = jnp.sum(jnp.where(chosen, my_scores, 0.0), axis=1)
    negative_score = jnp.max(jnp.where(chosen, -1e30, my_scores), axis=1)
    loss = jax.nn.softplus(negative_score - positive_score)
    return (hidden, patch_grad, weight_grad, my_scores, loss)


def solution(mesh):
    return jax.shard_map(
        body,
        mesh=mesh,
        in_specs=(
            P(("dp", "mp"), None),
            P(),
            P(None, "mp"),
            P(None, "mp"),
            P(),
            P("dp", None, None),
            P(),
            P("dp"),
            P(("dp", "mp"), None),
        ),
        out_specs=(
            P(("dp", "mp"), None),
            P(("dp", "mp"), None),
            P("dp", "mp"),
            P("dp", None),
            P("dp"),
        ),
        check_vma=False,
    )
```

```python
from functools import partial
import math

import jax
import jax.numpy as jnp
from jax import lax
from jax.experimental import pallas as pl
from jax.experimental.pallas import tpu as pltpu
from jax.sharding import PartitionSpec as P


HEAD_DIM = 72
LANES = 128
HEAD_LANES = 256
EMB = 128
QTOK = 32
MP = 4
DISTANCES = (4, 1, 2)
ARRIVAL = (0, 4, 1, 5, 2, 6, 3, 7)
SCALE = HEAD_DIM ** (-0.5)
LOG2E = math.log2(math.e)
F32 = jnp.float32
BF16 = jnp.bfloat16

HBM = pl.BlockSpec(memory_space=pltpu.HBM)
VMEM = pl.BlockSpec(memory_space=pltpu.VMEM)
SMEM = pl.BlockSpec(memory_space=pltpu.SMEM)


def dot(left, right, left_dim, right_dim):
    return lax.dot_general(
        left, right, (((left_dim,), (right_dim,)), ((), ())), preferred_element_type=F32
    )


def shape(dims, kind):
    return jax.ShapeDtypeStruct(dims, kind)


def cost(flops, size, exps=0):
    return pl.CostEstimate(flops=int(flops), bytes_accessed=int(size), transcendentals=int(exps))


def grant(mebibytes):
    return pltpu.CompilerParams(vmem_limit_bytes=mebibytes * 1024 * 1024)


def full(*dims):
    return pl.BlockSpec(dims, lambda *_: (0,) * len(dims))


def unit_rows(values):
    return values * lax.rsqrt(jnp.sum(values * values, axis=-1, keepdims=True) + 1e-06)


def place_of(index, model_index, rows_dev):
    return (model_index ^ (index // rows_dev)) * rows_dev + index % rows_dev


def gain_row(gain_ref):
    return jnp.concatenate([gain_ref[row : row + 1, :] for row in range(gain_ref.shape[0])], axis=1)


def norm_rows(block, gain):
    values = block.astype(F32)
    center = values - jnp.mean(values, axis=-1, keepdims=True)
    spread = jnp.mean(center * center, axis=-1, keepdims=True)
    return (center * lax.rsqrt(spread + 1e-06) * gain).astype(BF16)


def prepare_kernel(
    heads, rows_hbm, gain_hbm, mixing_hbm, output_hbm, rows1, mixing_pad, output_pad, packed_ref,
    rows0, gain_ref, mixing_ref, output_ref, normed, sems
):
    def spread(source, target, index, size, room):
        target[index * room : index * room + size, :] = source[index * size : (index + 1) * size, :]
        target[index * room + size : (index + 1) * room, :] = jnp.zeros(
            (room - size, target.shape[1]), BF16
        )

    sources = (rows_hbm, gain_hbm, mixing_hbm, output_hbm)
    targets = (rows0, gain_ref, mixing_ref, output_ref)
    fetches = [
        pltpu.make_async_copy(source, target, sems.at[index])
        for index, (source, target) in enumerate(zip(sources, targets))
    ]
    for fetch in fetches:
        fetch.start()
    fetches[0].wait()
    fetches[1].wait()
    size = rows0.shape[0]
    gain = gain_row(gain_ref)
    for index, block in enumerate((rows0, rows1)):
        normed[index * size : (index + 1) * size, :] = norm_rows(block[...], gain)
    fetches[2].wait()
    for index in range(heads):
        spread(mixing_ref, mixing_pad, index, 3 * HEAD_DIM, HEAD_LANES)
    fetches[3].wait()
    for index in range(heads):
        spread(output_ref, output_pad, index, HEAD_DIM, LANES)
    packed_ref[...] = dot(normed[...], mixing_pad[...], 1, 1).astype(BF16)


def in_hbm(values):
    return pltpu.with_memory_space_constraint(values, pltpu.HBM)


def prepare(mixing, output, rows0, rows1, gain, heads):
    width = mixing.shape[1]
    size = 2 * rows0.shape[0]
    return pl.pallas_call(
        partial(prepare_kernel, heads),
        out_shape=(
            shape((heads * HEAD_LANES, width), BF16),
            shape((heads * LANES, width), BF16),
            shape((size, heads * HEAD_LANES), BF16),
        ),
        in_specs=[HBM] * 4 + [VMEM],
        out_specs=(VMEM,) * 3,
        scratch_shapes=[
            pltpu.VMEM(rows0.shape, BF16),
            pltpu.VMEM(gain.shape, F32),
            pltpu.VMEM(mixing.shape, BF16),
            pltpu.VMEM(output.shape, BF16),
            pltpu.VMEM((size, width), BF16),
            pltpu.SemaphoreType.DMA((4,)),
        ],
        cost_estimate=cost(1e9, 8e6),
        name="prepare",
        compiler_params=grant(24),
    )(in_hbm(rows0), in_hbm(gain), in_hbm(mixing), in_hbm(output), rows1)


def head_parts(packed_ref, head):
    start = head * HEAD_LANES
    ends = [start + index * HEAD_DIM for index in range(4)]
    return [packed_ref[:, low:high] for low, high in zip(ends, ends[1:])]


def hand_out(product, keep0, keep2, send):
    size = keep0.shape[0]
    keep0[...] = product[:size].astype(BF16)
    send[:size, :] = product[size : 2 * size].astype(BF16)
    keep2[...] = product[2 * size : 3 * size].astype(BF16)
    send[size:, :] = product[3 * size :].astype(BF16)


def forward_kernel(
    heads,
    rows_dev,
    counts_ref,
    early_ref,
    rows2,
    rows3,
    gain_ref,
    mixing_ref,
    output_ref,
    packed_ref,
    prob_ref,
    attended_ref,
    keep0,
    keep2,
    send,
    normed,
):
    rows = rows_dev * MP
    gain = gain_row(gain_ref)
    for index, block in enumerate((rows2, rows3)):
        normed[index * rows_dev : (index + 1) * rows_dev, :] = norm_rows(block[...], gain)
    half = 2 * rows_dev
    packed_ref[:half, :] = early_ref[...]
    packed_ref[half:, :] = dot(normed[...], mixing_ref[...], 1, 1).astype(BF16)
    count = counts_ref[lax.axis_index("dp")]
    model_index = lax.axis_index("mp")
    columns = lax.broadcasted_iota(jnp.int32, (1, rows), 1)
    seen = place_of(columns, model_index, rows_dev) < count
    lines = lax.broadcasted_iota(jnp.int32, (rows, 1), 0)
    live = place_of(lines, model_index, rows_dev) < count
    for head in range(heads):
        query, key, value = head_parts(packed_ref, head)
        score = dot(query, key, 1, 1)
        score = jnp.where(seen, score, -1e30)
        largest = jnp.max(score, axis=-1, keepdims=True)
        raised = jnp.exp2((score - largest) * (SCALE * LOG2E))
        total = jnp.sum(raised, axis=-1, keepdims=True)
        prob = (raised * (1.0 / total)).astype(BF16)
        prob_ref[head] = prob
        found = dot(prob, value, 1, 0)
        start = head * LANES
        attended_ref[:, start : start + HEAD_DIM] = jnp.where(live, found, 0.0).astype(BF16)
        attended_ref[:, start + HEAD_DIM : start + LANES] = jnp.zeros(
            (rows, LANES - HEAD_DIM), BF16
        )
    hand_out(dot(attended_ref[...], output_ref[...], 1, 0), keep0, keep2, send)


def handed_shapes(rows_dev, width):
    kept = shape((rows_dev, width), BF16)
    return (kept, kept, shape((2 * rows_dev, width), BF16))


def forward(counts, early, blocks, gain, mixing_pad, output_pad, heads):
    rows_dev, width = blocks[0].shape
    rows = rows_dev * MP
    return pl.pallas_call(
        partial(forward_kernel, heads, rows_dev),
        out_shape=(
            shape((rows, heads * HEAD_LANES), BF16),
            shape((heads, rows, rows), BF16),
            shape((rows, heads * LANES), BF16),
        )
        + handed_shapes(rows_dev, width),
        in_specs=[SMEM] + [VMEM] * 6,
        out_specs=(VMEM,) * 6,
        scratch_shapes=[pltpu.VMEM((2 * rows_dev, width), BF16)],
        cost_estimate=cost(3e9, 12e6, heads * rows * rows),
        name="forward_attention",
        compiler_params=grant(28),
    )(counts, early, *blocks, gain, mixing_pad, output_pad)


def weight_kernel(
    heads, rows_dev, order, grad0, grad1, grad2, grad3, attended_ref, *refs
):
    (stacked, *outs), (result,) = refs[: len(refs) - 1], refs[len(refs) - 1 :]
    for index, block in enumerate((grad0, grad1, grad2, grad3)):
        stacked[index * rows_dev : (index + 1) * rows_dev, :] = block[...]
    product = dot(stacked[...], attended_ref[...], 0, 0)
    for index in range(heads):
        result[:, index * HEAD_DIM : (index + 1) * HEAD_DIM] = product[
            :, index * LANES : index * LANES + HEAD_DIM
        ]
    if order is None:
        outs[0][...] = result[...]
    else:
        mine = lax.axis_index("dp")
        share = result.shape[0] // sum(len(group) for group in order)
        for group, out in zip(order, outs):
            for spot, piece in enumerate(group):
                start = pl.multiple_of((mine ^ piece) * share, 16)
                out[spot * share : (spot + 1) * share, :] = result[
                    pl.ds(start, share), :
                ].astype(out.dtype)


def weight_parts(grads, attended, order):
    rows_dev, width = grads[0].shape
    heads = attended.shape[1] // LANES
    narrow = heads * HEAD_DIM
    if order is None:
        outs = (shape((width, narrow), F32),)
    else:
        share = width // sum(len(group) for group in order)
        outs = tuple(
            shape((len(group) * share, narrow), F32 if index == 0 else BF16)
            for index, group in enumerate(order)
        )
    outs = (shape((rows_dev * MP, width), BF16),) + outs
    return pl.pallas_call(
        partial(weight_kernel, heads, rows_dev, order),
        out_shape=outs,
        in_specs=[VMEM] * (MP + 1),
        out_specs=(VMEM,) * len(outs),
        scratch_shapes=[pltpu.VMEM((width, narrow), F32)],
        cost_estimate=cost(7e8, 4e6),
        name="weight_parts",
        compiler_params=grant(20),
    )(*grads, attended)


def backward_kernel(heads, counts_ref, stacked_ref, output_ref, packed_ref, prob_ref, out_ref):
    rows = stacked_ref.shape[0]
    count = counts_ref[lax.axis_index("dp")]
    lines = lax.broadcasted_iota(jnp.int32, (rows, 1), 0)
    live = place_of(lines, lax.axis_index("mp"), rows // MP) < count
    flows = dot(stacked_ref[...], output_ref[...], 1, 1)
    flows = jnp.where(live, flows, 0.0).astype(BF16)
    for head in range(heads):
        flow = flows[:, head * LANES : head * LANES + HEAD_DIM]
        query, key, value = head_parts(packed_ref, head)
        weights = prob_ref[head]
        prob = weights.astype(F32)
        grad_prob = dot(flow, value, 1, 1)
        delta = jnp.sum(grad_prob * prob, axis=-1, keepdims=True)
        grad_score = (prob * (grad_prob - delta)).astype(BF16)
        parts = (
            (dot(grad_score, key, 1, 0) * SCALE).astype(BF16),
            (dot(query, grad_score, 0, 0) * SCALE).T.astype(BF16),
            dot(flow, weights, 0, 0).T.astype(BF16),
            jnp.zeros((rows, HEAD_LANES - 3 * HEAD_DIM), BF16),
        )
        out_ref[:, head * HEAD_LANES : (head + 1) * HEAD_LANES] = jnp.concatenate(parts, axis=1)


def backward(counts, stacked, output_pad, packed, probs):
    heads, rows, _ = probs.shape
    return pl.pallas_call(
        partial(backward_kernel, heads),
        out_shape=shape((rows, heads * HEAD_LANES), BF16),
        in_specs=[SMEM] + [VMEM] * 4,
        out_specs=VMEM,
        cost_estimate=cost(4e9, 6e6),
        name="backward_attention",
        compiler_params=grant(28),
    )(counts, stacked, output_pad, packed, probs)


def branch_kernel(joined_ref, mixing_ref, keep0, keep2, send):
    hand_out(dot(joined_ref[...], mixing_ref[...], 1, 0), keep0, keep2, send)


def input_branch(joined, mixing_pad):
    return pl.pallas_call(
        branch_kernel,
        out_shape=handed_shapes(joined.shape[0] // MP, mixing_pad.shape[1]),
        in_specs=[VMEM] * 2,
        out_specs=(VMEM,) * 3,
        cost_estimate=cost(2e9, 8e6),
        name="input_branch",
        compiler_params=grant(24),
    )(joined, mixing_pad)


def score_kernel(
    rows_dev, few, counts_ref, patch_ref, part_ref, near_ref, far_ref, embed_ref, tokens_ref,
    hidden_ref, best_ref, page_emb
):
    mine = lax.axis_index("dp")

    def embed():
        near = near_ref[: part_ref.shape[0], :]
        mixed = part_ref[...].astype(F32) + near.astype(F32) + far_ref[...].astype(F32)
        hidden = (patch_ref[...].astype(F32) + mixed).astype(BF16)
        hidden_ref[...] = hidden
        embedded = dot(hidden, embed_ref[...], 1, 0)
        page_emb[...] = unit_rows(embedded).astype(BF16)

    if few:
        embed()
    else:
        pl.when(pl.program_id(0) == 0)(embed)
    tokens = unit_rows(tokens_ref[...].astype(F32)).astype(BF16)
    similar = dot(page_emb[...], tokens, 1, 1)
    lines = lax.broadcasted_iota(jnp.int32, (rows_dev, 1), 0) + lax.axis_index("mp") * rows_dev
    similar = jnp.where(lines < counts_ref[mine], similar, -2.0)
    best = jnp.max(similar, axis=0, keepdims=True)
    if few:
        size = best_ref.shape[1]
        for piece in range(best.shape[1] // size):
            row = best[:, piece * size : (piece + 1) * size]
            for copy in range(MP):
                best_ref[pl.ds((mine ^ ARRIVAL[piece]) * MP + copy, 1), :] = row
    else:
        best_ref[...] = best


def hidden_and_best(counts, patches, part, received, far, embed_weight, tokens, few, local):
    rows_dev, width = patches.shape
    size = tokens.shape[0]
    chunk = size if few else math.gcd(size, 1024)
    block = full(rows_dev, width)
    if few:
        best_shape = shape((size // local * MP, local), F32)
        layout = dict(in_specs=[SMEM] + [VMEM] * 6, out_specs=(VMEM, VMEM))
    else:
        best_shape = shape((1, size), F32)
        layout = dict(
            grid=(size // chunk,),
            in_specs=[SMEM]
            + [block] * 4
            + [full(width, EMB), pl.BlockSpec((chunk, EMB), lambda index: (index, 0))],
            out_specs=(block, pl.BlockSpec((1, chunk), lambda index: (0, index))),
        )
    return pl.pallas_call(
        partial(score_kernel, rows_dev, few),
        **layout,
        out_shape=(shape((rows_dev, width), BF16), best_shape),
        scratch_shapes=[pltpu.VMEM((rows_dev, EMB), BF16)],
        cost_estimate=cost(1e8, 2e6),
        name="hidden_and_best",
        compiler_params=grant(12),
    )(counts, patches, part, received, far, embed_weight, tokens)


def norm_back_kernel(patch_ref, gain_ref, grad_ref, part_ref, near_ref, far_ref, *refs):
    values = patch_ref[...].astype(F32)
    center = values - jnp.mean(values, axis=-1, keepdims=True)
    spread = jnp.mean(center * center, axis=-1, keepdims=True)
    inverse = lax.rsqrt(spread + 1e-06)
    near = near_ref[: part_ref.shape[0], :]
    flow = part_ref[...].astype(F32) + near.astype(F32) + far_ref[...].astype(F32)
    flow = flow * gain_row(gain_ref)
    along = jnp.mean(flow * center, axis=-1, keepdims=True)
    level = jnp.mean(flow, axis=-1, keepdims=True)
    result = inverse * (flow - level - center * (inverse * inverse * along))
    out = (grad_ref[...].astype(F32) + result).astype(BF16)
    if len(refs) == 1:
        refs[0][...] = out
        return
    mine_ref, other_ref, found_ref, positive_ref, out_ref, weight_ref, score_ref, loss_ref = refs
    out_ref[...] = out
    weight_ref[...] = mine_ref[...] + other_ref[...].astype(F32)
    pages = found_ref.shape[0] // MP
    best = jnp.max(found_ref[...].reshape(pages, MP, found_ref.shape[1]), axis=1)
    turned = best.T
    columns = lax.broadcasted_iota(jnp.int32, (1, pages), 1)
    for query in range(score_ref.shape[0]):
        row = jnp.sum(turned[query * QTOK : (query + 1) * QTOK], axis=0, keepdims=True)
        score_ref[query : query + 1, :] = row
        chosen = columns == positive_ref[query]
        positive = jnp.sum(jnp.where(chosen, row, 0.0), axis=1, keepdims=True)
        negative = jnp.max(jnp.where(chosen, -1e30, row), axis=1, keepdims=True)
        gap = negative - positive
        loss = jnp.maximum(gap, 0.0) + jnp.log1p(jnp.exp(-jnp.abs(gap)))
        loss_ref[query] = loss[0, 0]


def norm_back(patches, gain, grads, part, near, far, more=()):
    out_shape, out_specs, specs = [shape(patches.shape, BF16)], [VMEM], []
    if more:
        mine, _, found, positive = more
        scores = (positive.shape[0], found.shape[0] // MP)
        specs = [VMEM, VMEM, VMEM, SMEM]
        out_shape += [shape(mine.shape, F32), shape(scores, F32), shape(positive.shape, F32)]
        out_specs += [VMEM, VMEM, SMEM]
    return pl.pallas_call(
        norm_back_kernel,
        out_shape=tuple(out_shape),
        in_specs=[VMEM] * 6 + specs,
        out_specs=tuple(out_specs),
        cost_estimate=cost(3e6, 2e6),
        name="norm_back",
        compiler_params=grant(12),
    )(patches, gain, grads, part, near, far, *more)


def join_kernel(kept_ref, got1_ref, got2_ref, got3_ref, mine_ref, send_ref):
    share = mine_ref.shape[0]
    total = kept_ref[...]
    for ref in (got1_ref, got2_ref, got3_ref):
        total = total + ref[...].astype(F32)
    mine_ref[...] = total[:share]
    send_ref[...] = total[share:].astype(BF16)


def join_parts(kept, *got):
    share = (kept.shape[0] // 2, kept.shape[1])
    return pl.pallas_call(
        join_kernel,
        out_shape=(shape(share, F32), shape(share, BF16)),
        in_specs=[VMEM] * 4,
        out_specs=(VMEM,) * 2,
        cost_estimate=cost(3e5, 1e6),
        name="join_parts",
        compiler_params=grant(6),
    )(kept, *got)


def swap(values, axis, distance):
    size = lax.axis_size(axis)
    return lax.ppermute(values, axis, [(index, index ^ distance) for index in range(size)])


def scatter_sum(parts):
    part0, part2, send = parts
    received = swap(send, "mp", 1)
    relayed = received[part2.shape[0] :]
    going = (part2.astype(F32) + relayed.astype(F32)).astype(BF16)
    return part0, received, swap(going, "mp", 2), going


def after(values, *others):
    return lax.optimization_barrier((values, *others))[0]


def body(
    patches,
    norm_gain,
    query_key_value,
    output_weight,
    embed_weight,
    query_tokens,
    patch_counts,
    positive_page,
    hidden_grad,
):
    data_index = lax.axis_index("dp")
    data_size = lax.axis_size("dp")
    few = data_size == 8
    heads = output_weight.shape[1] // HEAD_DIM
    gain = norm_gain.reshape(-1, LANES)

    rows2 = swap(patches, "mp", 2)
    rows1 = swap(patches, "mp", 1)
    grads2 = swap(hidden_grad, "mp", 2)
    grads1 = swap(hidden_grad, "mp", 1)

    local = query_tokens.shape[0]
    own_tokens = query_tokens.reshape(local * QTOK, EMB)
    mixing_pad, output_pad, early = prepare(
        query_key_value.T, output_weight.T, patches, rows1, gain, heads
    )
    if few:
        tokens = own_tokens
        for distance in DISTANCES[:2]:
            other = swap(tokens, "dp", distance)
            tokens = jnp.concatenate([tokens, other], axis=0)
    else:
        tokens = lax.all_gather(own_tokens, "dp", axis=0, tiled=True)
    rows2 = after(rows2, early)
    rows3 = swap(rows2, "mp", 1)

    packed, probs, attended, *parts = forward(
        patch_counts, early, (rows2, rows3), gain, mixing_pad, output_pad, heads
    )
    grads3 = swap(after(grads2, rows3), "mp", 1)
    grads = (hidden_grad, grads1, grads2, grads3)
    part, received, far, _ = scatter_sum(parts)
    if few:
        order = ((0, 4), (1, 5), (2, 6), (3, 7))
        stacked, kept, *sent_parts = weight_parts(grads, attended, order)
        got = [swap(values, "dp", index + 1) for index, values in enumerate(sent_parts)]
        other = swap(tokens, "dp", 2)
        near_tokens = tokens
        joined = backward(patch_counts, stacked, output_pad, packed, probs)
        tokens = jnp.concatenate([after(near_tokens, joined), after(other, joined)], axis=0)
    else:
        stacked, whole = weight_parts(grads, attended, None)
        weight_grad = lax.psum_scatter(whole, "dp", scatter_dimension=0, tiled=True)
        joined = backward(patch_counts, stacked, output_pad, packed, probs)
    hidden, best = hidden_and_best(
        patch_counts, patches, part, received, far, embed_weight, tokens, few, local * QTOK
    )
    if few:
        joined, best = lax.optimization_barrier((joined, best))
    grad_parts = input_branch(joined, mixing_pad)
    part, received, far, sent = scatter_sum(grad_parts)
    more = ()
    if few:
        mine, send = join_parts(kept, *got)
        other = swap(send, "dp", 4)
        found = lax.all_to_all(after(best, sent), ("dp", "mp"), 0, 0, tiled=True)
        more = (mine, other, found, positive_page)
    patch_grad, *rest = norm_back(patches, gain, hidden_grad, part, received, far, more)
    if few:
        return (hidden, patch_grad, *rest)
    best = jnp.maximum(best, swap(best, "mp", 1))
    best = jnp.maximum(best, swap(best, "mp", 2))
    part_scores = jnp.sum(best.reshape(-1, QTOK), axis=1)
    every = lax.all_gather(part_scores.reshape(-1, 1), "dp", axis=1, tiled=True)
    my_scores = lax.dynamic_slice_in_dim(every, data_index * local, local, 0)
    columns = jnp.arange(my_scores.shape[1], dtype=jnp.int32)
    chosen = columns[None, :] == positive_page[:, None]
    positive_score = jnp.sum(jnp.where(chosen, my_scores, 0.0), axis=1)
    negative_score = jnp.max(jnp.where(chosen, -1e30, my_scores), axis=1)
    loss = jax.nn.softplus(negative_score - positive_score)
    return (hidden, patch_grad, weight_grad, my_scores, loss)


def solution(mesh):
    return jax.shard_map(
        body,
        mesh=mesh,
        in_specs=(
            P(("dp", "mp"), None),
            P(),
            P(None, "mp"),
            P(None, "mp"),
            P(),
            P("dp", None, None),
            P(),
            P("dp"),
            P(("dp", "mp"), None),
        ),
        out_specs=(
            P(("dp", "mp"), None),
            P(("dp", "mp"), None),
            P("dp", "mp"),
            P("dp", None),
            P("dp"),
        ),
        check_vma=False,
    )
```

```python
from functools import partial
import math

import jax
import jax.numpy as jnp
from jax import lax
from jax.experimental import pallas as pl
from jax.experimental.pallas import tpu as pltpu
from jax.sharding import PartitionSpec as P


HEAD_DIM = 72
LANES = 128
HEAD_LANES = 256
EMB = 128
QTOK = 32
MP = 4
DISTANCES = (4, 1, 2)
SCALE = HEAD_DIM ** (-0.5)
LOG2E = math.log2(math.e)
F32 = jnp.float32
BF16 = jnp.bfloat16

HBM = pl.BlockSpec(memory_space=pltpu.HBM)
VMEM = pl.BlockSpec(memory_space=pltpu.VMEM)
SMEM = pl.BlockSpec(memory_space=pltpu.SMEM)


def dot(left, right, left_dim, right_dim):
    return lax.dot_general(
        left, right, (((left_dim,), (right_dim,)), ((), ())), preferred_element_type=F32
    )


def shape(dims, kind):
    return jax.ShapeDtypeStruct(dims, kind)


def cost(flops, size, exps=0):
    return pl.CostEstimate(flops=int(flops), bytes_accessed=int(size), transcendentals=int(exps))


def grant(mebibytes):
    return pltpu.CompilerParams(vmem_limit_bytes=mebibytes * 1024 * 1024)


def full(*dims):
    return pl.BlockSpec(dims, lambda *_: (0,) * len(dims))


def unit_rows(values):
    return values * lax.rsqrt(jnp.sum(values * values, axis=-1, keepdims=True) + 1e-06)


def place_of(index, model_index, rows_dev):
    return (model_index ^ (index // rows_dev)) * rows_dev + index % rows_dev


def gain_row(gain_ref):
    return jnp.concatenate([gain_ref[row : row + 1, :] for row in range(gain_ref.shape[0])], axis=1)


def norm_rows(block, gain):
    values = block.astype(F32)
    center = values - jnp.mean(values, axis=-1, keepdims=True)
    spread = jnp.mean(center * center, axis=-1, keepdims=True)
    return (center * lax.rsqrt(spread + 1e-06) * gain).astype(BF16)


def prepare_kernel(
    heads, rows_hbm, gain_hbm, mixing_hbm, output_hbm, rows1, mixing_pad, output_pad, packed_ref,
    rows0, gain_ref, mixing_ref, output_ref, normed, sems
):
    def spread(source, target, index, size, room):
        target[index * room : index * room + size, :] = source[index * size : (index + 1) * size, :]
        target[index * room + size : (index + 1) * room, :] = jnp.zeros(
            (room - size, target.shape[1]), BF16
        )

    sources = (rows_hbm, gain_hbm, mixing_hbm, output_hbm)
    targets = (rows0, gain_ref, mixing_ref, output_ref)
    fetches = [
        pltpu.make_async_copy(source, target, sems.at[index])
        for index, (source, target) in enumerate(zip(sources, targets))
    ]
    for fetch in fetches:
        fetch.start()
    fetches[0].wait()
    fetches[1].wait()
    size = rows0.shape[0]
    gain = gain_row(gain_ref)
    for index, block in enumerate((rows0, rows1)):
        normed[index * size : (index + 1) * size, :] = norm_rows(block[...], gain)
    fetches[2].wait()
    for index in range(heads):
        spread(mixing_ref, mixing_pad, index, 3 * HEAD_DIM, HEAD_LANES)
    fetches[3].wait()
    for index in range(heads):
        spread(output_ref, output_pad, index, HEAD_DIM, LANES)
    packed_ref[...] = dot(normed[...], mixing_pad[...], 1, 1).astype(BF16)


def in_hbm(values):
    return pltpu.with_memory_space_constraint(values, pltpu.HBM)


def prepare(mixing, output, rows0, rows1, gain, heads):
    width = mixing.shape[1]
    size = 2 * rows0.shape[0]
    return pl.pallas_call(
        partial(prepare_kernel, heads),
        out_shape=(
            shape((heads * HEAD_LANES, width), BF16),
            shape((heads * LANES, width), BF16),
            shape((size, heads * HEAD_LANES), BF16),
        ),
        in_specs=[HBM] * 4 + [VMEM],
        out_specs=(VMEM,) * 3,
        scratch_shapes=[
            pltpu.VMEM(rows0.shape, BF16),
            pltpu.VMEM(gain.shape, F32),
            pltpu.VMEM(mixing.shape, BF16),
            pltpu.VMEM(output.shape, BF16),
            pltpu.VMEM((size, width), BF16),
            pltpu.SemaphoreType.DMA((4,)),
        ],
        cost_estimate=cost(1e9, 8e6),
        name="prepare",
        compiler_params=grant(24),
    )(in_hbm(rows0), in_hbm(gain), in_hbm(mixing), in_hbm(output), rows1)


def head_parts(packed_ref, head):
    start = head * HEAD_LANES
    ends = [start + index * HEAD_DIM for index in range(4)]
    return [packed_ref[:, low:high] for low, high in zip(ends, ends[1:])]


def hand_out(product, keep0, keep2, send):
    size = keep0.shape[0]
    keep0[...] = product[:size].astype(BF16)
    send[:size, :] = product[size : 2 * size].astype(BF16)
    keep2[...] = product[2 * size : 3 * size].astype(BF16)
    send[size:, :] = product[3 * size :].astype(BF16)


def forward_kernel(
    heads,
    rows_dev,
    counts_ref,
    early_ref,
    rows2,
    rows3,
    gain_ref,
    mixing_ref,
    output_ref,
    packed_ref,
    prob_ref,
    attended_ref,
    keep0,
    keep2,
    send,
    normed,
):
    rows = rows_dev * MP
    gain = gain_row(gain_ref)
    for index, block in enumerate((rows2, rows3)):
        normed[index * rows_dev : (index + 1) * rows_dev, :] = norm_rows(block[...], gain)
    half = 2 * rows_dev
    packed_ref[:half, :] = early_ref[...]
    packed_ref[half:, :] = dot(normed[...], mixing_ref[...], 1, 1).astype(BF16)
    count = counts_ref[lax.axis_index("dp")]
    model_index = lax.axis_index("mp")
    columns = lax.broadcasted_iota(jnp.int32, (1, rows), 1)
    seen = place_of(columns, model_index, rows_dev) < count
    lines = lax.broadcasted_iota(jnp.int32, (rows, 1), 0)
    live = place_of(lines, model_index, rows_dev) < count
    for head in range(heads):
        query, key, value = head_parts(packed_ref, head)
        score = dot(query, key, 1, 1)
        score = jnp.where(seen, score, -1e30)
        largest = jnp.max(score, axis=-1, keepdims=True)
        raised = jnp.exp2((score - largest) * (SCALE * LOG2E))
        total = jnp.sum(raised, axis=-1, keepdims=True)
        prob = (raised * (1.0 / total)).astype(BF16)
        prob_ref[head] = prob
        found = dot(prob, value, 1, 0)
        start = head * LANES
        attended_ref[:, start : start + HEAD_DIM] = jnp.where(live, found, 0.0).astype(BF16)
        attended_ref[:, start + HEAD_DIM : start + LANES] = jnp.zeros(
            (rows, LANES - HEAD_DIM), BF16
        )
    hand_out(dot(attended_ref[...], output_ref[...], 1, 0), keep0, keep2, send)


def handed_shapes(rows_dev, width):
    kept = shape((rows_dev, width), BF16)
    return (kept, kept, shape((2 * rows_dev, width), BF16))


def forward(counts, early, blocks, gain, mixing_pad, output_pad, heads):
    rows_dev, width = blocks[0].shape
    rows = rows_dev * MP
    return pl.pallas_call(
        partial(forward_kernel, heads, rows_dev),
        out_shape=(
            shape((rows, heads * HEAD_LANES), BF16),
            shape((heads, rows, rows), BF16),
            shape((rows, heads * LANES), BF16),
        )
        + handed_shapes(rows_dev, width),
        in_specs=[SMEM] + [VMEM] * 6,
        out_specs=(VMEM,) * 6,
        scratch_shapes=[pltpu.VMEM((2 * rows_dev, width), BF16)],
        cost_estimate=cost(3e9, 12e6, heads * rows * rows),
        name="forward_attention",
        compiler_params=grant(28),
    )(counts, early, *blocks, gain, mixing_pad, output_pad)


def weight_kernel(
    heads, rows_dev, order, grad0, grad1, grad2, grad3, attended_ref, *refs
):
    (stacked, *outs), (result,) = refs[: len(refs) - 1], refs[len(refs) - 1 :]
    for index, block in enumerate((grad0, grad1, grad2, grad3)):
        stacked[index * rows_dev : (index + 1) * rows_dev, :] = block[...]
    product = dot(stacked[...], attended_ref[...], 0, 0)
    for index in range(heads):
        result[:, index * HEAD_DIM : (index + 1) * HEAD_DIM] = product[
            :, index * LANES : index * LANES + HEAD_DIM
        ]
    if order is None:
        outs[0][...] = result[...]
    else:
        mine = lax.axis_index("dp")
        share = result.shape[0] // sum(len(group) for group in order)
        for group, out in zip(order, outs):
            for spot, piece in enumerate(group):
                start = pl.multiple_of((mine ^ piece) * share, 16)
                out[spot * share : (spot + 1) * share, :] = result[
                    pl.ds(start, share), :
                ].astype(out.dtype)


def weight_parts(grads, attended, order):
    rows_dev, width = grads[0].shape
    heads = attended.shape[1] // LANES
    narrow = heads * HEAD_DIM
    if order is None:
        outs = (shape((width, narrow), F32),)
    else:
        share = width // sum(len(group) for group in order)
        outs = tuple(
            shape((len(group) * share, narrow), F32 if index == 0 else BF16)
            for index, group in enumerate(order)
        )
    outs = (shape((rows_dev * MP, width), BF16),) + outs
    return pl.pallas_call(
        partial(weight_kernel, heads, rows_dev, order),
        out_shape=outs,
        in_specs=[VMEM] * (MP + 1),
        out_specs=(VMEM,) * len(outs),
        scratch_shapes=[pltpu.VMEM((width, narrow), F32)],
        cost_estimate=cost(7e8, 4e6),
        name="weight_parts",
        compiler_params=grant(20),
    )(*grads, attended)


def backward_kernel(heads, counts_ref, stacked_ref, output_ref, packed_ref, prob_ref, out_ref):
    rows = stacked_ref.shape[0]
    count = counts_ref[lax.axis_index("dp")]
    lines = lax.broadcasted_iota(jnp.int32, (rows, 1), 0)
    live = place_of(lines, lax.axis_index("mp"), rows // MP) < count
    flows = dot(stacked_ref[...], output_ref[...], 1, 1)
    flows = jnp.where(live, flows, 0.0).astype(BF16)
    for head in range(heads):
        flow = flows[:, head * LANES : head * LANES + HEAD_DIM]
        query, key, value = head_parts(packed_ref, head)
        weights = prob_ref[head]
        prob = weights.astype(F32)
        grad_prob = dot(flow, value, 1, 1)
        delta = jnp.sum(grad_prob * prob, axis=-1, keepdims=True)
        grad_score = (prob * (grad_prob - delta)).astype(BF16)
        parts = (
            (dot(grad_score, key, 1, 0) * SCALE).astype(BF16),
            (dot(query, grad_score, 0, 0) * SCALE).T.astype(BF16),
            dot(flow, weights, 0, 0).T.astype(BF16),
            jnp.zeros((rows, HEAD_LANES - 3 * HEAD_DIM), BF16),
        )
        out_ref[:, head * HEAD_LANES : (head + 1) * HEAD_LANES] = jnp.concatenate(parts, axis=1)


def backward(counts, stacked, output_pad, packed, probs):
    heads, rows, _ = probs.shape
    return pl.pallas_call(
        partial(backward_kernel, heads),
        out_shape=shape((rows, heads * HEAD_LANES), BF16),
        in_specs=[SMEM] + [VMEM] * 4,
        out_specs=VMEM,
        cost_estimate=cost(4e9, 6e6),
        name="backward_attention",
        compiler_params=grant(28),
    )(counts, stacked, output_pad, packed, probs)


def branch_kernel(joined_ref, mixing_ref, keep0, keep2, send):
    hand_out(dot(joined_ref[...], mixing_ref[...], 1, 0), keep0, keep2, send)


def input_branch(joined, mixing_pad):
    return pl.pallas_call(
        branch_kernel,
        out_shape=handed_shapes(joined.shape[0] // MP, mixing_pad.shape[1]),
        in_specs=[VMEM] * 2,
        out_specs=(VMEM,) * 3,
        cost_estimate=cost(2e9, 8e6),
        name="input_branch",
        compiler_params=grant(24),
    )(joined, mixing_pad)


def score_kernel(
    rows_dev, few, counts_ref, patch_ref, part_ref, near_ref, far_ref, embed_ref, tokens_ref,
    hidden_ref, best_ref, page_emb
):
    mine = lax.axis_index("dp")

    def embed():
        near = near_ref[: part_ref.shape[0], :]
        mixed = part_ref[...].astype(F32) + near.astype(F32) + far_ref[...].astype(F32)
        hidden = (patch_ref[...].astype(F32) + mixed).astype(BF16)
        hidden_ref[...] = hidden
        embedded = dot(hidden, embed_ref[...], 1, 0)
        page_emb[...] = unit_rows(embedded).astype(BF16)

    if few:
        embed()
    else:
        pl.when(pl.program_id(0) == 0)(embed)
    tokens = unit_rows(tokens_ref[...].astype(F32)).astype(BF16)
    similar = dot(page_emb[...], tokens, 1, 1)
    lines = lax.broadcasted_iota(jnp.int32, (rows_dev, 1), 0) + lax.axis_index("mp") * rows_dev
    similar = jnp.where(lines < counts_ref[mine], similar, -2.0)
    best = jnp.max(similar, axis=0, keepdims=True)
    if few:
        size = best_ref.shape[2]
        for piece in range(best.shape[1] // size):
            best_ref[piece // 2, piece % 2 : piece % 2 + 1, :] = best[
                :, piece * size : (piece + 1) * size
            ]
    else:
        best_ref[...] = best


def hidden_and_best(counts, patches, part, received, far, embed_weight, tokens, few, local):
    rows_dev, width = patches.shape
    size = tokens.shape[0]
    chunk = size if few else math.gcd(size, 1024)
    block = full(rows_dev, width)
    if few:
        best_shape = shape((size // local // 2, 2, local), F32)
        layout = dict(in_specs=[SMEM] + [VMEM] * 6, out_specs=(VMEM, VMEM))
    else:
        best_shape = shape((1, size), F32)
        layout = dict(
            grid=(size // chunk,),
            in_specs=[SMEM]
            + [block] * 4
            + [full(width, EMB), pl.BlockSpec((chunk, EMB), lambda index: (index, 0))],
            out_specs=(block, pl.BlockSpec((1, chunk), lambda index: (0, index))),
        )
    return pl.pallas_call(
        partial(score_kernel, rows_dev, few),
        **layout,
        out_shape=(shape((rows_dev, width), BF16), best_shape),
        scratch_shapes=[pltpu.VMEM((rows_dev, EMB), BF16)],
        cost_estimate=cost(1e8, 2e6),
        name="hidden_and_best",
        compiler_params=grant(12),
    )(counts, patches, part, received, far, embed_weight, tokens)


def norm_back_kernel(patch_ref, gain_ref, grad_ref, part_ref, near_ref, far_ref, *refs):
    values = patch_ref[...].astype(F32)
    center = values - jnp.mean(values, axis=-1, keepdims=True)
    spread = jnp.mean(center * center, axis=-1, keepdims=True)
    inverse = lax.rsqrt(spread + 1e-06)
    near = near_ref[: part_ref.shape[0], :]
    flow = part_ref[...].astype(F32) + near.astype(F32) + far_ref[...].astype(F32)
    flow = flow * gain_row(gain_ref)
    along = jnp.mean(flow * center, axis=-1, keepdims=True)
    level = jnp.mean(flow, axis=-1, keepdims=True)
    result = inverse * (flow - level - center * (inverse * inverse * along))
    out = (grad_ref[...].astype(F32) + result).astype(BF16)
    if len(refs) == 1:
        refs[0][...] = out
        return
    mine_ref, other_ref, here_ref, one_ref, two_ref, three_ref, there_ref, positive_ref = refs[:8]
    out_ref, weight_ref, score_ref, loss_ref, found_ref = refs[8:]
    out_ref[...] = out
    weight_ref[...] = mine_ref[...] + other_ref[...].astype(F32)
    pages = found_ref.shape[0]
    near = (here_ref, one_ref, two_ref, three_ref)
    for index, ref in enumerate(near):
        found_ref[index : index + 1, :] = ref[0, :1, :]
    found_ref[len(near) :, :] = there_ref[...]
    own = lax.axis_index("dp")
    rows = [found_ref[pl.ds(page ^ own, 1), :] for page in range(pages)]
    turned = jnp.concatenate(rows, axis=0).T
    columns = lax.broadcasted_iota(jnp.int32, (1, pages), 1)
    for query in range(score_ref.shape[0]):
        row = jnp.sum(turned[query * QTOK : (query + 1) * QTOK], axis=0, keepdims=True)
        score_ref[query : query + 1, :] = row
        chosen = columns == positive_ref[query]
        positive = jnp.sum(jnp.where(chosen, row, 0.0), axis=1, keepdims=True)
        negative = jnp.max(jnp.where(chosen, -1e30, row), axis=1, keepdims=True)
        gap = negative - positive
        loss = jnp.maximum(gap, 0.0) + jnp.log1p(jnp.exp(-jnp.abs(gap)))
        loss_ref[query] = loss[0, 0]


def norm_back(patches, gain, grads, part, near, far, more=()):
    out_shape, out_specs, specs = [shape(patches.shape, BF16)], [VMEM], []
    scratch = []
    if more:
        mine, positive, there = more[0], more[-1], more[-2]
        pages = 2 * there.shape[0]
        scores = (positive.shape[0], pages)
        specs = [VMEM] * 7 + [SMEM]
        out_shape += [shape(mine.shape, F32), shape(scores, F32), shape(positive.shape, F32)]
        out_specs += [VMEM, VMEM, SMEM]
        scratch = [pltpu.VMEM((pages, there.shape[1]), F32)]
    return pl.pallas_call(
        norm_back_kernel,
        out_shape=tuple(out_shape),
        in_specs=[VMEM] * 6 + specs,
        out_specs=tuple(out_specs),
        scratch_shapes=scratch,
        cost_estimate=cost(3e6, 2e6),
        name="norm_back",
        compiler_params=grant(12),
    )(patches, gain, grads, part, near, far, *more)


def join_kernel(kept_ref, got1_ref, got2_ref, got3_ref, mine_ref, send_ref):
    share = mine_ref.shape[0]
    total = kept_ref[...]
    for ref in (got1_ref, got2_ref, got3_ref):
        total = total + ref[...].astype(F32)
    mine_ref[...] = total[:share]
    send_ref[...] = total[share:].astype(BF16)


def join_parts(kept, *got):
    share = (kept.shape[0] // 2, kept.shape[1])
    return pl.pallas_call(
        join_kernel,
        out_shape=(shape(share, F32), shape(share, BF16)),
        in_specs=[VMEM] * 4,
        out_specs=(VMEM,) * 2,
        cost_estimate=cost(3e5, 1e6),
        name="join_parts",
        compiler_params=grant(6),
    )(kept, *got)


def swap(values, axis, distance):
    size = lax.axis_size(axis)
    return lax.ppermute(values, axis, [(index, index ^ distance) for index in range(size)])


def scatter_sum(parts):
    part0, part2, send = parts
    received = swap(send, "mp", 1)
    relayed = received[part2.shape[0] :]
    going = (part2.astype(F32) + relayed.astype(F32)).astype(BF16)
    return part0, received, swap(going, "mp", 2), going


def after(values, *others):
    return lax.optimization_barrier((values, *others))[0]


def body(
    patches,
    norm_gain,
    query_key_value,
    output_weight,
    embed_weight,
    query_tokens,
    patch_counts,
    positive_page,
    hidden_grad,
):
    data_index = lax.axis_index("dp")
    data_size = lax.axis_size("dp")
    few = data_size == 8
    heads = output_weight.shape[1] // HEAD_DIM
    gain = norm_gain.reshape(-1, LANES)

    rows2 = swap(patches, "mp", 2)
    rows1 = swap(patches, "mp", 1)
    grads2 = swap(hidden_grad, "mp", 2)
    grads1 = swap(hidden_grad, "mp", 1)

    local = query_tokens.shape[0]
    own_tokens = query_tokens.reshape(local * QTOK, EMB)
    mixing_pad, output_pad, early = prepare(
        query_key_value.T, output_weight.T, patches, rows1, gain, heads
    )
    if few:
        tokens = own_tokens
        for distance in DISTANCES[:2]:
            other = swap(tokens, "dp", distance)
            tokens = jnp.concatenate([tokens, other], axis=0)
    else:
        tokens = lax.all_gather(own_tokens, "dp", axis=0, tiled=True)
    rows2 = after(rows2, early)
    rows3 = swap(rows2, "mp", 1)

    packed, probs, attended, *parts = forward(
        patch_counts, early, (rows2, rows3), gain, mixing_pad, output_pad, heads
    )
    grads3 = swap(after(grads2, rows3), "mp", 1)
    grads = (hidden_grad, grads1, grads2, grads3)
    part, received, far, _ = scatter_sum(parts)
    if few:
        order = ((0, 4), (1, 5), (2, 6), (3, 7))
        stacked, kept, *sent_parts = weight_parts(grads, attended, order)
        got = [swap(values, "dp", index + 1) for index, values in enumerate(sent_parts)]
        other = swap(tokens, "dp", 2)
        near_tokens = tokens
        joined = backward(patch_counts, stacked, output_pad, packed, probs)
        tokens = jnp.concatenate([after(near_tokens, joined), after(other, joined)], axis=0)
    else:
        stacked, whole = weight_parts(grads, attended, None)
        weight_grad = lax.psum_scatter(whole, "dp", scatter_dimension=0, tiled=True)
        joined = backward(patch_counts, stacked, output_pad, packed, probs)
    hidden, best = hidden_and_best(
        patch_counts, patches, part, received, far, embed_weight, tokens, few, local * QTOK
    )
    if few:
        joined, best = lax.optimization_barrier((joined, best))
        best = jnp.maximum(best, swap(best, "mp", 1))
        best = jnp.maximum(best, swap(best, "mp", 2))
    grad_parts = input_branch(joined, mixing_pad)
    part, received, far, _ = scatter_sum(grad_parts)
    more = ()
    if few:
        mine, send = join_parts(kept, *got)
        other = swap(send, "dp", 4)
        best = after(best, send)
        found = [best[:1]] + [swap(best[index : index + 1], "dp", index) for index in (1, 2, 3)]
        going = jnp.concatenate([part[0, 1:] for part in found], axis=0)
        there = swap(going, "dp", 4)
        more = (mine, other, *found, there, positive_page)
    patch_grad, *rest = norm_back(patches, gain, hidden_grad, part, received, far, more)
    if few:
        return (hidden, patch_grad, *rest)
    best = jnp.maximum(best, swap(best, "mp", 1))
    best = jnp.maximum(best, swap(best, "mp", 2))
    part_scores = jnp.sum(best.reshape(-1, QTOK), axis=1)
    every = lax.all_gather(part_scores.reshape(-1, 1), "dp", axis=1, tiled=True)
    my_scores = lax.dynamic_slice_in_dim(every, data_index * local, local, 0)
    columns = jnp.arange(my_scores.shape[1], dtype=jnp.int32)
    chosen = columns[None, :] == positive_page[:, None]
    positive_score = jnp.sum(jnp.where(chosen, my_scores, 0.0), axis=1)
    negative_score = jnp.max(jnp.where(chosen, -1e30, my_scores), axis=1)
    loss = jax.nn.softplus(negative_score - positive_score)
    return (hidden, patch_grad, weight_grad, my_scores, loss)


def solution(mesh):
    return jax.shard_map(
        body,
        mesh=mesh,
        in_specs=(
            P(("dp", "mp"), None),
            P(),
            P(None, "mp"),
            P(None, "mp"),
            P(),
            P("dp", None, None),
            P(),
            P("dp"),
            P(("dp", "mp"), None),
        ),
        out_specs=(
            P(("dp", "mp"), None),
            P(("dp", "mp"), None),
            P("dp", "mp"),
            P("dp", None),
            P("dp"),
        ),
        check_vma=False,
    )
```
